32 devices in a mesh: mode: 16 (over z, y, x), real: 2 (over core).
Axes of the slice: x: 2, y: 2, z: 4, core: 2. Of those that a mesh axis runs over, the one named last changes fastest.
Arguments:
- input_field: bfloat16 [2, 2, 256, 16384], P(None, 'real', 'mode'), may hold values from -6 to 6
- kerr_coeff: bfloat16 [16, 64, 64], P('mode'), may hold values from -0.375 to 0.375
- block_list: int32 [16, 4], P('mode'), may hold values from 0 to 31
Outputs:
- density: float32 [512, 2, 256, 256], P('mode', None, 'real')
The draws below stay inside these ranges and needn't reach their ends.
All inputs are finite; a program needn't handle non-finite values.
Results may differ from the reference program's by a relative error of at most 0.0085.
Values may be sent and summed in bfloat16 or wider, within the bound.
A program may use at most 64 MiB of HBM per device.

```python
import jax
import jax.numpy as jnp
from jax import lax

P_SIZE = 256
MB = 8
FT = 128
NB = 512
R_DEV = 1
NT = 16384
NMB = 32
FB = 32
NBLK = 16
RE = 2
N_REAL = 2


def with_ends(values, rng, smallest, top_value):
    longest = values.shape.index(max(values.shape))
    spots = []
    for shift in (0, 1):
        where = [jax.random.randint(jax.random.fold_in(rng, axis), (), 0, length) for axis, length in enumerate(values.shape)]
        where[longest] = (where[longest] + shift) % values.shape[longest]
        spots.append(tuple(where))
    return values.at[spots[0]].set(smallest).at[spots[1]].set(top_value)


def levels(stream_key, dims, split, least, largest):
    factor_of = 1.0
    for axis_at, parts in split:
        steps = jax.random.uniform(jax.random.fold_in(jax.random.fold_in(stream_key, 6), axis_at), (parts,), jnp.float32, least / len(split), largest / len(split))
        factor_of = factor_of * jnp.repeat(jnp.exp(steps), dims[axis_at] // parts).reshape((-1,) + (1,) * (len(dims) - 1 - axis_at))
    return factor_of


def normal_values(stream_key, shape, spread, limit, pieces=(), kind=jnp.bfloat16):
    drawn = spread * jax.random.normal(stream_key, shape, jnp.float32)
    if pieces:
        drawn = drawn * levels(stream_key, shape, pieces, -0.22, 0.18)
    return jnp.clip(drawn, -limit, limit).astype(kind)


def setup_inputs(seed: int = 0) -> dict:
    arg_keys = jax.random.split(jax.random.key(seed), 4)
    input_field = normal_values(arg_keys[0], (2, RE, P_SIZE, NT), 1.0, 6.0, ((1, 2), (2, 16)))
    kerr_coeff = normal_values(arg_keys[1], (NBLK, MB * MB, MB * MB), (16 * NBLK) ** -0.5, 0.375, ((0, 16),))
    block_list = with_ends(jax.random.randint(arg_keys[2], (NBLK, 4), 0, NMB), jax.random.fold_in(arg_keys[2], 1), 0, NMB - 1).astype(jnp.int32)
    return dict(input_field=input_field, kerr_coeff=kerr_coeff, block_list=block_list)


kerr_strength = 0.25


def band_product(rows_part, cols_part):
    return jnp.einsum("rpbf,rqbf->bpq", rows_part.astype(jnp.float32), cols_part.astype(jnp.float32), precision=lax.Precision.HIGHEST)


def reference(input_field, kerr_coeff, block_list):
    total_real = R_DEV * N_REAL
    field_blocks = input_field.reshape(2, total_real, NMB, MB, NT)

    def add_block(running, item):
        coeff_one, block_one = item
        mode_l = lax.dynamic_index_in_dim(field_blocks, block_one[1], 2, keepdims=False).astype(jnp.float32)
        mode_m = lax.dynamic_index_in_dim(field_blocks, block_one[2], 2, keepdims=False).astype(jnp.float32)
        mode_n = lax.dynamic_index_in_dim(field_blocks, block_one[3], 2, keepdims=False).astype(jnp.float32)
        prod_re = mode_m[0][:, :, None, :] * mode_n[0][:, None, :, :] + mode_m[1][:, :, None, :] * mode_n[1][:, None, :, :]
        prod_im = mode_m[1][:, :, None, :] * mode_n[0][:, None, :, :] - mode_m[0][:, :, None, :] * mode_n[1][:, None, :, :]
        pairs = jnp.stack([prod_re, prod_im]).reshape(2, total_real, MB * MB, NT).astype(jnp.bfloat16)
        weighted = jnp.einsum("ab,crbt->crat", coeff_one.astype(jnp.float32), pairs.astype(jnp.float32), precision=lax.Precision.HIGHEST)
        weighted = weighted.reshape(2, total_real, MB, MB, NT)
        term_re = jnp.sum(weighted[0] * mode_l[0][:, None] - weighted[1] * mode_l[1][:, None], axis=2)
        term_im = jnp.sum(weighted[0] * mode_l[1][:, None] + weighted[1] * mode_l[0][:, None], axis=2)
        target = block_one[0]
        before = lax.dynamic_index_in_dim(running, target, 2, keepdims=False)
        running = lax.dynamic_update_index_in_dim(running, before + jnp.stack([term_re, term_im]), target, 2)
        return running, None

    initial = jnp.zeros((2, total_real, NMB, MB, NT), jnp.float32)
    kerr_sum, unused = lax.scan(add_block, initial, (kerr_coeff, block_list))
    kerr_sum = kerr_sum.reshape(2, total_real, P_SIZE, NT)
    base = input_field.astype(jnp.float32)
    stepped_re = (base[0] - kerr_strength * kerr_sum[1]).astype(jnp.bfloat16)
    stepped_im = (base[1] + kerr_strength * kerr_sum[0]).astype(jnp.bfloat16)
    spectrum = jnp.fft.fft(lax.complex(stepped_re.astype(jnp.float32), stepped_im.astype(jnp.float32)), axis=-1) / FT
    spec_re = lax.optimization_barrier(jnp.real(spectrum).astype(jnp.bfloat16))
    spec_im = lax.optimization_barrier(jnp.imag(spectrum).astype(jnp.bfloat16))
    band_re = spec_re.reshape(total_real, P_SIZE, NB, FB)
    band_im = spec_im.reshape(total_real, P_SIZE, NB, FB)
    dens_re = band_product(band_re, band_re) + band_product(band_im, band_im)
    dens_im = band_product(band_im, band_re) - band_product(band_re, band_im)
    return jnp.stack([dens_re, dens_im], axis=1) / (FB * total_real)
```

```python
import functools
import math

import jax
import jax.numpy as jnp
import numpy as np
from jax import lax
from jax.experimental import pallas as pl
from jax.experimental.pallas import tpu as pltpu
from jax.sharding import PartitionSpec as P

MB = 8
FT = 128
NT = 16384
FB = 32


kerr_strength = 0.25


def kerr_terms(field_blocks, coeff_group, block_group):
    mode_l = jnp.take(field_blocks, block_group[:, 1], axis=2).astype(jnp.float32)
    mode_m = jnp.take(field_blocks, block_group[:, 2], axis=2).astype(jnp.float32)
    mode_n = jnp.take(field_blocks, block_group[:, 3], axis=2).astype(jnp.float32)
    realiz = field_blocks.shape[1]
    group_size = block_group.shape[0]
    steps_local = field_blocks.shape[4]
    prod_re = (
        mode_m[0][:, :, :, None, :] * mode_n[0][:, :, None, :, :]
        + mode_m[1][:, :, :, None, :] * mode_n[1][:, :, None, :, :]
    )
    prod_im = (
        mode_m[1][:, :, :, None, :] * mode_n[0][:, :, None, :, :]
        - mode_m[0][:, :, :, None, :] * mode_n[1][:, :, None, :, :]
    )
    pairs = (
        jnp.stack([prod_re, prod_im])
        .reshape(2, realiz, group_size, MB * MB, steps_local)
        .astype(jnp.bfloat16)
    )
    weighted = jnp.einsum(
        "kab,crkbt->crkat", coeff_group, pairs, preferred_element_type=jnp.float32
    )
    weighted = weighted.reshape(2, realiz, group_size, MB, MB, steps_local)
    term_re = jnp.sum(
        weighted[0] * mode_l[0][:, :, None] - weighted[1] * mode_l[1][:, :, None], axis=3
    )
    term_im = jnp.sum(
        weighted[0] * mode_l[1][:, :, None] + weighted[1] * mode_l[0][:, :, None], axis=3
    )
    one_hot = (
        block_group[:, 0][:, None] == jnp.arange(field_blocks.shape[2], dtype=jnp.int32)[None, :]
    ).astype(jnp.float32)
    return jnp.einsum(
        "kg,crkpt->crgpt", one_hot, jnp.stack([term_re, term_im]), precision=lax.Precision.HIGHEST
    )


def phase_table(extent, modulus):
    index_a = jnp.arange(extent, dtype=jnp.int32)[:, None]
    index_b = jnp.arange(extent, dtype=jnp.int32)[None, :]
    angle = 2.0 * math.pi / modulus * (index_a * index_b % modulus).astype(jnp.float32)
    return (jnp.cos(angle), -jnp.sin(angle))


def first_pass(table, data):
    table_high = table.astype(jnp.bfloat16)
    table_low = (table - table_high.astype(jnp.float32)).astype(jnp.bfloat16)
    upper = jnp.einsum("kn,rmnj->rmkj", table_high, data, preferred_element_type=jnp.float32)
    return upper + jnp.einsum("kn,rmnj->rmkj", table_low, data, preferred_element_type=jnp.float32)


def second_pass(table, data):
    return jnp.einsum("jn,rmkn->rmjk", table, data, precision=lax.Precision.HIGH)


def transform(by_mode):
    realiz = by_mode.shape[1]
    local_modes = by_mode.shape[2]
    signal = by_mode.reshape(2, realiz, local_modes, FT, FT)
    four_re, four_im = phase_table(FT, FT)
    twist_re, twist_im = phase_table(FT, NT)
    half_re = first_pass(four_re, signal[0]) - first_pass(four_im, signal[1])
    half_im = first_pass(four_re, signal[1]) + first_pass(four_im, signal[0])
    turned_re = half_re * twist_re - half_im * twist_im
    turned_im = half_re * twist_im + half_im * twist_re
    out_re = (second_pass(four_re, turned_re) - second_pass(four_im, turned_im)) / FT
    out_im = (second_pass(four_re, turned_im) + second_pass(four_im, turned_re)) / FT
    return jnp.stack([out_re, out_im]).astype(jnp.bfloat16)


def gram_parts(rows_part, cols_part):
    quarters = jnp.einsum(
        "crpbf,drqbf->bcdpq", rows_part, cols_part, preferred_element_type=jnp.float32
    )
    return jnp.stack(
        [quarters[:, 0, 0] + quarters[:, 1, 1], quarters[:, 1, 0] - quarters[:, 0, 1]], axis=1
    )


def shards(input_field, kerr_coeff, block_list):
    timed = lax.all_to_all(input_field, "mode", split_axis=3, concat_axis=2, tiled=True)
    realiz = timed.shape[1]
    width = timed.shape[2]
    steps_local = timed.shape[3]
    field_blocks = timed.reshape(2, realiz, width // MB, MB, steps_local)
    initial = jnp.zeros(field_blocks.shape, jnp.float32)
    running = initial
    coeff_piece = lax.all_gather(kerr_coeff, "mode", axis=0, tiled=True)
    block_piece = lax.all_gather(block_list, "mode", axis=0, tiled=True)
    block_count = block_piece.shape[0]
    coeff_groups = coeff_piece.reshape(
        block_count // 8, 8, coeff_piece.shape[1], coeff_piece.shape[2]
    )
    block_groups = block_piece.reshape(block_count // 8, 8, 4)

    def one_group(carried, groups):
        return (carried + kerr_terms(field_blocks, groups[0], groups[1]), None)

    running, unused = lax.scan(one_group, running, (coeff_groups, block_groups))
    kerr_sum = running
    kerr_sum = kerr_sum.reshape(2, realiz, width, steps_local)
    base = timed.astype(jnp.float32)
    stepped = jnp.stack(
        [base[0] - kerr_strength * kerr_sum[1], base[1] + kerr_strength * kerr_sum[0]]
    ).astype(jnp.bfloat16)
    by_mode = lax.all_to_all(stepped, "mode", split_axis=2, concat_axis=3, tiled=True)
    spectrum = transform(by_mode)
    banded = lax.all_to_all(spectrum, "mode", split_axis=3, concat_axis=2, tiled=True)
    bands_dev = banded.shape[3] * FT // FB
    spec_bands = banded.reshape(2, realiz, width, bands_dev, FB)
    scale = 1.0 / (FB * realiz * lax.axis_size("real"))
    row_count = width // lax.axis_size("real")
    row_first = lax.axis_index("real") * row_count
    shard_piece = lax.all_gather(spec_bands, "real", axis=1, tiled=True)
    own_part = lax.dynamic_slice_in_dim(shard_piece, row_first, row_count, 2)
    return gram_parts(own_part, shard_piece) * scale


VMEM = pltpu.VMEM
BIG = 60 * 1024 * 1024


def spread_kernel(parts, x_ref, coef_ref, list_ref, x_out, coef_out, list_out, sends, recvs, own):
    me = lax.axis_index("mode")
    steps = x_ref.shape[2] // parts
    barrier = pltpu.get_barrier_semaphore()
    for step in range(1, parts):
        pl.semaphore_signal(
            barrier,
            inc=1,
            device_id={"mode": lax.rem(me + step, parts)},
            device_id_type=pl.DeviceIdType.MESH,
        )
    pl.semaphore_wait(barrier, parts - 1)
    copies = []
    for step in range(1, parts):
        to = lax.rem(me + step, parts)
        chunk = pl.ds(pl.multiple_of(to * steps, 128), steps)
        pairs = (
            (coef_ref, coef_out.at[me]),
            (list_ref, list_out.at[me]),
            (x_ref.at[:, :, chunk], x_out.at[me]),
        )
        for slot, (here, there) in enumerate(pairs):
            copy = pltpu.make_async_remote_copy(
                src_ref=here,
                dst_ref=there,
                send_sem=sends.at[step, slot],
                recv_sem=recvs.at[step, slot],
                device_id={"mode": to},
                device_id_type=pl.DeviceIdType.MESH,
            )
            copy.start()
            copies.append(copy)
    chunk = pl.ds(pl.multiple_of(me * steps, 128), steps)
    pairs = (
        (coef_ref, coef_out.at[me]),
        (list_ref, list_out.at[me]),
        (x_ref.at[:, :, chunk], x_out.at[me]),
    )
    for slot, (here, there) in enumerate(pairs):
        copy = pltpu.make_async_copy(here, there, own.at[slot])
        copy.start()
        copies.append(copy)
    for copy in copies:
        copy.wait()


def spread(field, coef, listed, parts):
    two, modes, times = field.shape
    return pl.pallas_call(
        functools.partial(spread_kernel, parts),
        out_shape=(
            jax.ShapeDtypeStruct((parts, two, modes, times // parts), field.dtype),
            jax.ShapeDtypeStruct((parts,) + coef.shape, coef.dtype),
            jax.ShapeDtypeStruct((parts,) + listed.shape, listed.dtype),
        ),
        in_specs=[pl.BlockSpec(memory_space=VMEM)] * 3,
        out_specs=(pl.BlockSpec(memory_space=VMEM),) * 3,
        scratch_shapes=[
            pltpu.SemaphoreType.DMA((parts, 3)),
            pltpu.SemaphoreType.DMA((parts, 3)),
            pltpu.SemaphoreType.DMA((3,)),
        ],
        compiler_params=pltpu.CompilerParams(collective_id=0, has_side_effects=True),
    )(field, coef, listed)


def kerr_kernel(list_ref, field_ref, coef_ref, out_ref, fld, acc, rows):
    parts, _, modes, steps = field_ref.shape
    groups = fld.shape[1]
    blocks = coef_ref.shape[0]
    fine = steps // FT
    piece = min(steps, 256)
    for c in range(2):
        fld[c] = field_ref[:, c].astype(jnp.float32).reshape(groups, MB, steps)
    acc[...] = jnp.zeros_like(acc)

    def one_block(k, carry):
        to, bl, bm, bn = (list_ref[k, i] for i in range(4))
        coef = coef_ref[k]
        for first in range(0, steps, piece):
            span = pl.ds(first, piece)
            m_re, m_im = fld[0, bm, :, span][:, None], fld[1, bm, :, span][:, None]
            n_re, n_im = fld[0, bn, :, span][None], fld[1, bn, :, span][None]
            p_re = (m_re * n_re + m_im * n_im).reshape(MB * MB, piece)
            p_im = (m_im * n_re - m_re * n_im).reshape(MB * MB, piece)
            pairs = jnp.concatenate([p_re, p_im], axis=1).astype(jnp.bfloat16)
            w = jnp.dot(coef, pairs, preferred_element_type=jnp.float32)
            w_re = w[:, :piece].reshape(MB, MB, piece)
            w_im = w[:, piece:].reshape(MB, MB, piece)
            l_re, l_im = fld[0, bl, :, span][:, None], fld[1, bl, :, span][:, None]
            acc[0, to, :, span] += jnp.sum(w_re * l_re - w_im * l_im, axis=0)
            acc[1, to, :, span] += jnp.sum(w_re * l_im + w_im * l_re, axis=0)
        return carry

    lax.fori_loop(0, blocks, one_block, 0)

    def one_group(g, carry):
        new = (
            fld[0, g] - kerr_strength * acc[1, g],
            fld[1, g] + kerr_strength * acc[0, g],
        )
        for c in range(2):
            for n in range(fine):
                at = pl.ds(g * (MB * 2 * fine) + c * fine + n, MB, stride=2 * fine)
                rows[at, :] = new[c][:, n * FT : (n + 1) * FT]
        return carry

    lax.fori_loop(0, groups, one_group, 0)
    out_ref[...] = rows[...].astype(jnp.bfloat16)


def kerr_step(listed, timed, coef):
    parts, _, modes, steps = timed.shape
    width = parts * modes
    count = width * 2 * steps // FT
    return pl.pallas_call(
        kerr_kernel,
        out_shape=jax.ShapeDtypeStruct((count, FT), jnp.bfloat16),
        in_specs=[
            pl.BlockSpec(memory_space=pltpu.SMEM),
            pl.BlockSpec(memory_space=VMEM),
            pl.BlockSpec(memory_space=VMEM),
        ],
        out_specs=pl.BlockSpec(memory_space=VMEM),
        scratch_shapes=[
            VMEM((2, width // MB, MB, steps), jnp.float32),
            VMEM((2, width // MB, MB, steps), jnp.float32),
            VMEM((count, FT), jnp.float32),
        ],
        compiler_params=pltpu.CompilerParams(vmem_limit_bytes=BIG),
    )(listed, timed, coef)


def dft_tables(parts):
    a = np.arange(FT)
    four = np.exp(-2j * np.pi / FT * (np.outer(a, a) % FT))
    twist = np.exp(-2j * np.pi / NT * (np.outer(a, a) % NT)) / FT
    real = np.block([[four.real, -four.imag], [four.imag, four.real]])
    first = real.reshape(2 * FT, 2, parts, FT // parts).transpose(0, 2, 1, 3)
    first = first.reshape(2 * FT, 2 * FT)
    second = real.reshape(2, FT, 2 * FT).transpose(1, 0, 2).reshape(2 * FT, 2 * FT)

    def split(t):
        t = t.astype(np.float32)
        high = t.astype(jnp.bfloat16)
        return high, (t - high.astype(np.float32)).astype(jnp.bfloat16)

    return (
        *split(first),
        twist.real.astype(np.float32),
        twist.imag.astype(np.float32),
        *split(second),
    )


def dft_kernel(x_ref, f1h, f1l, tw_re, tw_im, f2h, f2l, out_ref, rows):
    modes = x_ref.shape[1]
    nt = (((1,), (1,)), ((), ()))
    dot = functools.partial(jnp.dot, preferred_element_type=jnp.float32)
    dot_nt = functools.partial(
        lax.dot_general, dimension_numbers=nt, preferred_element_type=jnp.float32
    )
    for m in range(0, modes, 2):
        x = jnp.concatenate(
            [x_ref[:, m].reshape(2 * FT, FT), x_ref[:, m + 1].reshape(2 * FT, FT)], axis=1
        )
        half = dot(f1h[...], x) + dot(f1l[...], x)
        turned = []
        for i in range(2):
            h_re, h_im = half[:FT, i * FT : (i + 1) * FT], half[FT:, i * FT : (i + 1) * FT]
            turned.append(
                jnp.concatenate(
                    [
                        h_re * tw_re[...] - h_im * tw_im[...],
                        h_re * tw_im[...] + h_im * tw_re[...],
                    ],
                    axis=1,
                )
            )
        turned = jnp.concatenate(turned, axis=0)
        high = turned.astype(jnp.bfloat16)
        low = (turned - high.astype(jnp.float32)).astype(jnp.bfloat16)
        out = dot_nt(f2h[...], high) + dot_nt(f2h[...], low) + dot_nt(f2l[...], high)
        for i in range(2):
            rows[pl.ds(m + i, 2 * FT, stride=modes), :] = out[:, i * FT : (i + 1) * FT]
    out_ref[...] = rows[...].astype(jnp.bfloat16)


def dft(by_mode):
    parts, modes, _, _ = by_mode.shape
    tables = dft_tables(parts)
    return pl.pallas_call(
        dft_kernel,
        out_shape=jax.ShapeDtypeStruct((2 * FT * modes, FT), jnp.bfloat16),
        in_specs=[pl.BlockSpec(memory_space=VMEM)] * 7,
        out_specs=pl.BlockSpec(memory_space=VMEM),
        scratch_shapes=[VMEM((2 * FT * modes, FT), jnp.float32)],
        compiler_params=pltpu.CompilerParams(vmem_limit_bytes=BIG),
    )(by_mode, *tables)


def gram_kernel(scale, half_ref, *refs):
    *spec_refs, out_ref = refs
    parts, _, _, modes, _ = spec_refs[0].shape
    row_count = out_ref.shape[2]
    sources = row_count // modes
    first = half_ref[0] * sources
    cols, rows_re, rows_im = [], [], []
    for ref in spec_refs:
        re, im = (ref[:, 0, c].reshape(parts * modes, FT) for c in range(2))
        own = pl.ds(first, sources)
        own_re, own_im = (ref[own, 0, c].reshape(row_count, FT) for c in range(2))
        cols += [re, im]
        rows_re += [own_re, own_im]
        rows_im += [own_im, -own_re]
    cols = jnp.concatenate(cols, axis=1)
    rows = jnp.concatenate(
        [jnp.concatenate(rows_re, axis=1), jnp.concatenate(rows_im, axis=1)], axis=0
    )
    lane = lax.broadcasted_iota(jnp.int32, rows.shape, 1)
    band = (lane % FT) // FB
    for g in range(FT // FB):
        kept = jnp.where(band == g, rows, jnp.zeros_like(rows))
        out = lax.dot_general(
            kept, cols, (((1,), (1,)), ((), ())), preferred_element_type=jnp.float32
        )
        out_ref[g] = (out * scale).reshape(2, row_count, parts * modes)


def gram(half, spectra, row_count, scale):
    parts, high, _, modes, _ = spectra[0].shape
    width = parts * modes
    per = FT // FB
    return pl.pallas_call(
        functools.partial(gram_kernel, scale),
        grid=(high,),
        out_shape=jax.ShapeDtypeStruct((high * per, 2, row_count, width), jnp.float32),
        in_specs=[pl.BlockSpec(memory_space=pltpu.SMEM)]
        + [pl.BlockSpec((parts, 1, 2, modes, FT), lambda j: (0, j, 0, 0, 0))] * len(spectra),
        out_specs=pl.BlockSpec((per, 2, row_count, width), lambda j: (j, 0, 0, 0)),
        compiler_params=pltpu.CompilerParams(vmem_limit_bytes=BIG),
    )(half, *spectra)


def tiled_shards(input_field, kerr_coeff, block_list):
    parts, sides = lax.axis_size("mode"), lax.axis_size("real")
    _, _, modes, times = input_field.shape
    width = parts * modes
    fine = FT // parts
    coef = kerr_coeff[0].reshape(MB, MB, MB * MB).transpose(1, 0, 2).reshape(MB * MB, MB * MB)
    listed = jnp.pad(block_list, ((0, 7), (0, FT - block_list.shape[1])))
    timed, coefs, lists = spread(input_field.reshape(2, modes, times), coef, listed, parts)
    stepped = kerr_step(lists[:, 0, :4], timed, coefs)
    stepped = stepped.reshape(parts, modes, 2 * fine, FT)
    by_mode = lax.all_to_all(stepped, "mode", split_axis=0, concat_axis=0)
    spectrum = dft(by_mode).reshape(parts, fine, 2, modes, FT)
    own = lax.all_to_all(spectrum, "mode", split_axis=0, concat_axis=0)
    ring = [(i, (i + 1) % sides) for i in range(sides)]
    spectra = [own]
    for _ in range(sides - 1):
        spectra.append(lax.ppermute(spectra[-1], "real", ring))
    half = lax.axis_index("real").astype(jnp.int32).reshape(1)
    return gram(half, spectra, width // sides, 1.0 / (FB * sides))


def tiles_fit(mesh):
    parts = mesh.shape["mode"]
    return FT % parts == 0 and (2 * FT // parts) % 16 == 0 and mesh.shape["real"] <= 2


def either(mesh, input_field, kerr_coeff, block_list):
    modes = input_field.shape[2]
    blocks_each = kerr_coeff.shape[0]
    fits = tiles_fit(mesh) and modes % 16 == 0 and blocks_each == 1
    fits = fits and input_field.shape[1] == 1 and input_field.shape[3] == NT
    return (tiled_shards if fits else shards)(input_field, kerr_coeff, block_list)


def solution(mesh):
    return jax.shard_map(
        functools.partial(either, mesh),
        mesh=mesh,
        in_specs=(P(None, "real", "mode", None), P("mode", None, None), P("mode", None)),
        out_specs=P("mode", None, "real", None),
        check_vma=False,
    )
```

```python
import functools
import math

import jax
import jax.numpy as jnp
import numpy as np
from jax import lax
from jax.experimental import pallas as pl
from jax.experimental.pallas import tpu as pltpu
from jax.sharding import PartitionSpec as P

MB = 8
FT = 128
NT = 16384
FB = 32


kerr_strength = 0.25


def kerr_terms(field_blocks, coeff_group, block_group):
    mode_l = jnp.take(field_blocks, block_group[:, 1], axis=2).astype(jnp.float32)
    mode_m = jnp.take(field_blocks, block_group[:, 2], axis=2).astype(jnp.float32)
    mode_n = jnp.take(field_blocks, block_group[:, 3], axis=2).astype(jnp.float32)
    realiz = field_blocks.shape[1]
    group_size = block_group.shape[0]
    steps_local = field_blocks.shape[4]
    prod_re = (
        mode_m[0][:, :, :, None, :] * mode_n[0][:, :, None, :, :]
        + mode_m[1][:, :, :, None, :] * mode_n[1][:, :, None, :, :]
    )
    prod_im = (
        mode_m[1][:, :, :, None, :] * mode_n[0][:, :, None, :, :]
        - mode_m[0][:, :, :, None, :] * mode_n[1][:, :, None, :, :]
    )
    pairs = (
        jnp.stack([prod_re, prod_im])
        .reshape(2, realiz, group_size, MB * MB, steps_local)
        .astype(jnp.bfloat16)
    )
    weighted = jnp.einsum(
        "kab,crkbt->crkat", coeff_group, pairs, preferred_element_type=jnp.float32
    )
    weighted = weighted.reshape(2, realiz, group_size, MB, MB, steps_local)
    term_re = jnp.sum(
        weighted[0] * mode_l[0][:, :, None] - weighted[1] * mode_l[1][:, :, None], axis=3
    )
    term_im = jnp.sum(
        weighted[0] * mode_l[1][:, :, None] + weighted[1] * mode_l[0][:, :, None], axis=3
    )
    one_hot = (
        block_group[:, 0][:, None] == jnp.arange(field_blocks.shape[2], dtype=jnp.int32)[None, :]
    ).astype(jnp.float32)
    return jnp.einsum(
        "kg,crkpt->crgpt", one_hot, jnp.stack([term_re, term_im]), precision=lax.Precision.HIGHEST
    )


def phase_table(extent, modulus):
    index_a = jnp.arange(extent, dtype=jnp.int32)[:, None]
    index_b = jnp.arange(extent, dtype=jnp.int32)[None, :]
    angle = 2.0 * math.pi / modulus * (index_a * index_b % modulus).astype(jnp.float32)
    return (jnp.cos(angle), -jnp.sin(angle))


def first_pass(table, data):
    table_high = table.astype(jnp.bfloat16)
    table_low = (table - table_high.astype(jnp.float32)).astype(jnp.bfloat16)
    upper = jnp.einsum("kn,rmnj->rmkj", table_high, data, preferred_element_type=jnp.float32)
    return upper + jnp.einsum("kn,rmnj->rmkj", table_low, data, preferred_element_type=jnp.float32)


def second_pass(table, data):
    return jnp.einsum("jn,rmkn->rmjk", table, data, precision=lax.Precision.HIGH)


def transform(by_mode):
    realiz = by_mode.shape[1]
    local_modes = by_mode.shape[2]
    signal = by_mode.reshape(2, realiz, local_modes, FT, FT)
    four_re, four_im = phase_table(FT, FT)
    twist_re, twist_im = phase_table(FT, NT)
    half_re = first_pass(four_re, signal[0]) - first_pass(four_im, signal[1])
    half_im = first_pass(four_re, signal[1]) + first_pass(four_im, signal[0])
    turned_re = half_re * twist_re - half_im * twist_im
    turned_im = half_re * twist_im + half_im * twist_re
    out_re = (second_pass(four_re, turned_re) - second_pass(four_im, turned_im)) / FT
    out_im = (second_pass(four_re, turned_im) + second_pass(four_im, turned_re)) / FT
    return jnp.stack([out_re, out_im]).astype(jnp.bfloat16)


def gram_parts(rows_part, cols_part):
    quarters = jnp.einsum(
        "crpbf,drqbf->bcdpq", rows_part, cols_part, preferred_element_type=jnp.float32
    )
    return jnp.stack(
        [quarters[:, 0, 0] + quarters[:, 1, 1], quarters[:, 1, 0] - quarters[:, 0, 1]], axis=1
    )


def shards(input_field, kerr_coeff, block_list):
    timed = lax.all_to_all(input_field, "mode", split_axis=3, concat_axis=2, tiled=True)
    realiz = timed.shape[1]
    width = timed.shape[2]
    steps_local = timed.shape[3]
    field_blocks = timed.reshape(2, realiz, width // MB, MB, steps_local)
    initial = jnp.zeros(field_blocks.shape, jnp.float32)
    running = initial
    coeff_piece = lax.all_gather(kerr_coeff, "mode", axis=0, tiled=True)
    block_piece = lax.all_gather(block_list, "mode", axis=0, tiled=True)
    block_count = block_piece.shape[0]
    coeff_groups = coeff_piece.reshape(
        block_count // 8, 8, coeff_piece.shape[1], coeff_piece.shape[2]
    )
    block_groups = block_piece.reshape(block_count // 8, 8, 4)

    def one_group(carried, groups):
        return (carried + kerr_terms(field_blocks, groups[0], groups[1]), None)

    running, unused = lax.scan(one_group, running, (coeff_groups, block_groups))
    kerr_sum = running
    kerr_sum = kerr_sum.reshape(2, realiz, width, steps_local)
    base = timed.astype(jnp.float32)
    stepped = jnp.stack(
        [base[0] - kerr_strength * kerr_sum[1], base[1] + kerr_strength * kerr_sum[0]]
    ).astype(jnp.bfloat16)
    by_mode = lax.all_to_all(stepped, "mode", split_axis=2, concat_axis=3, tiled=True)
    spectrum = transform(by_mode)
    banded = lax.all_to_all(spectrum, "mode", split_axis=3, concat_axis=2, tiled=True)
    bands_dev = banded.shape[3] * FT // FB
    spec_bands = banded.reshape(2, realiz, width, bands_dev, FB)
    scale = 1.0 / (FB * realiz * lax.axis_size("real"))
    row_count = width // lax.axis_size("real")
    row_first = lax.axis_index("real") * row_count
    shard_piece = lax.all_gather(spec_bands, "real", axis=1, tiled=True)
    own_part = lax.dynamic_slice_in_dim(shard_piece, row_first, row_count, 2)
    return gram_parts(own_part, shard_piece) * scale


VMEM = pltpu.VMEM
BIG = 60 * 1024 * 1024


def step_order(parts):
    return sorted(range(1, parts), key=lambda step: (-min(step, parts - step), step))


def remote(here, there, sent, landed, target):
    copy = pltpu.make_async_remote_copy(
        src_ref=here,
        dst_ref=there,
        send_sem=sent,
        recv_sem=landed,
        device_id=target,
        device_id_type=pl.DeviceIdType.MESH,
    )
    copy.start()
    return copy


def kerr_terms_at(first, piece, k, list_s, coef, fld, terms):
    span = pl.ds(first, piece)
    bl, bm, bn = (list_s[k, 0, i] for i in (1, 2, 3))
    m_re, m_im = fld[0, bm, :, span][:, None], fld[1, bm, :, span][:, None]
    n_re, n_im = fld[0, bn, :, span][None], fld[1, bn, :, span][None]
    p_re = (m_re * n_re + m_im * n_im).reshape(MB * MB, piece)
    p_im = (m_im * n_re - m_re * n_im).reshape(MB * MB, piece)
    pairs = jnp.concatenate([p_re, p_im], axis=1).astype(jnp.bfloat16)
    w = jnp.dot(coef, pairs, preferred_element_type=jnp.float32)
    w_re = w[:, :piece].reshape(MB, MB, piece)
    w_im = w[:, piece:].reshape(MB, MB, piece)
    l_re, l_im = fld[0, bl, :, span][:, None], fld[1, bl, :, span][:, None]
    at = pl.ds(pl.multiple_of(k * MB, MB), MB)
    terms[0, at, span] = jnp.sum(w_re * l_re - w_im * l_im, axis=0)
    terms[1, at, span] = jnp.sum(w_re * l_im + w_im * l_re, axis=0)


def owner_table(blocks, width, list_s):
    shape = (width, blocks * MB)
    row = lax.broadcasted_iota(jnp.int32, shape, 0)
    col = lax.broadcasted_iota(jnp.int32, shape, 1)
    wanted = jnp.full(shape, -1, jnp.int32)
    for k in range(blocks):
        wanted = jnp.where(col // MB == k, list_s[k, 0, 0] * MB + col % MB, wanted)
    return (row == wanted).astype(jnp.float32).astype(jnp.bfloat16)


def whole_kernel(parts, sides, x_ref, coef_ref, list_ref, f1h, f1l, tw_re, tw_im, f2h, f2l,
                 out_ref, timed, coefs, lists, list_s, fld, terms, rows, stepped, by_mode, spec,
                 sends, recvs, own_sems):
    me = lax.axis_index("mode")
    other = {"real": 1 - lax.axis_index("real")}
    _, modes, times = x_ref.shape
    steps = times // parts
    width = parts * modes
    groups = width // MB
    fine = steps // FT
    half = steps // 2
    piece = min(half, 256)
    order = step_order(parts)
    barrier = pltpu.get_barrier_semaphore()
    for step in order:
        to = {"mode": lax.rem(me + step, parts)}
        pl.semaphore_signal(barrier, inc=1, device_id=to, device_id_type=pl.DeviceIdType.MESH)
    if sides > 1:
        pl.semaphore_signal(barrier, inc=1, device_id=other, device_id_type=pl.DeviceIdType.MESH)
    pl.semaphore_wait(barrier, parts - 1 + (sides > 1))

    def chunk(to, part):
        at = pl.multiple_of(to * steps + part * half, 128)
        return x_ref.at[:, :, pl.ds(at, half)]

    def landing(part):
        return timed.at[me, :, :, pl.ds(part * half, half)]

    small, first, later = [], [], []
    for step in order:
        to = lax.rem(me + step, parts)
        there = {"mode": to}
        small.append(remote(coef_ref, coefs.at[me], sends.at[0, step], recvs.at[0, step], there))
        small.append(remote(list_ref, lists.at[me], sends.at[1, step], recvs.at[1, step], there))
    for part, copies in ((0, first), (1, later)):
        for step in order:
            to = lax.rem(me + step, parts)
            copies.append(
                remote(
                    chunk(to, part),
                    landing(part),
                    sends.at[2 + part, step],
                    recvs.at[2 + part, step],
                    {"mode": to},
                )
            )
    for slot, (here, there) in enumerate(
        (
            (coef_ref, coefs.at[me]),
            (list_ref, lists.at[me]),
            (chunk(me, 0), landing(0)),
            (chunk(me, 1), landing(1)),
        )
    ):
        copy = pltpu.make_async_copy(here, there, own_sems.at[slot])
        copy.start()
        (small, small, first, later)[slot].append(copy)
    for copy in small:
        copy.wait()
    copy = pltpu.make_async_copy(lists, list_s, own_sems.at[4])
    copy.start()
    copy.wait()
    blocks = coefs.shape[0]
    owners = owner_table(blocks, width, list_s)
    for part, copies in ((0, first), (1, later)):
        for copy in copies:
            copy.wait()
        span = pl.ds(part * half, half)
        for c in range(2):
            fld[c, :, :, span] = timed[:, c, :, span].astype(jnp.float32).reshape(groups, MB, half)

        def one_block(k, carry):
            coef = coefs[k]
            for at in range(part * half, (part + 1) * half, piece):
                kerr_terms_at(at, piece, k, list_s, coef, fld, terms)
            return carry

        lax.fori_loop(0, blocks, one_block, 0)
        for c in range(2):
            term = terms[1 - c, :, span]
            high = term.astype(jnp.bfloat16)
            low = (term - high.astype(jnp.float32)).astype(jnp.bfloat16)
            kerr = jnp.dot(owners, high, preferred_element_type=jnp.float32)
            kerr = kerr + jnp.dot(owners, low, preferred_element_type=jnp.float32)
            turn = kerr_strength * (2 * c - 1)
            new = fld[c, :, :, span].reshape(width, half) + turn * kerr
            for g in range(groups):
                for n in range(half // FT):
                    row = g * (MB * 2 * fine) + c * fine + part * (half // FT) + n
                    rows[pl.ds(row, MB, stride=2 * fine), :] = new[
                        g * MB : (g + 1) * MB, n * FT : (n + 1) * FT
                    ]
    stepped[...] = rows[...].astype(jnp.bfloat16).reshape(stepped.shape)

    pending = []
    for step in order:
        to = lax.rem(me + step, parts)
        pending.append(
            remote(stepped.at[to], by_mode.at[me], sends.at[4, step], recvs.at[4, step], {"mode": to})
        )
    copy = pltpu.make_async_copy(stepped.at[me], by_mode.at[me], own_sems.at[5])
    copy.start()
    for copy in pending + [copy]:
        copy.wait()

    dft_kernel(by_mode, f1h, f1l, tw_re, tw_im, f2h, f2l, rows)
    spec[...] = rows[...].astype(jnp.bfloat16).reshape(spec.shape)

    pending, passed = [], []
    for step in order:
        to = lax.rem(me + step, parts)
        pending.append(
            (
                remote(spec.at[to], out_ref.at[0, me], sends.at[5, step], recvs.at[5, step], {"mode": to}),
                lax.rem(me - step + parts, parts),
            )
        )
    copy = pltpu.make_async_copy(spec.at[me], out_ref.at[0, me], own_sems.at[6])
    copy.start()
    if sides > 1:
        passed.append(remote(spec.at[me], out_ref.at[1, me], sends.at[6, 0], recvs.at[6, 0], other))
    for step, (arrival, source) in zip(order, pending):
        arrival.wait_recv()
        if sides > 1:
            passed.append(
                remote(
                    out_ref.at[0, source],
                    out_ref.at[1, source],
                    sends.at[6, step],
                    recvs.at[6, step],
                    other,
                )
            )
    copy.wait()
    for arrival, _ in pending:
        arrival.wait_send()
    for copy in passed:
        copy.wait()


def spectra_of(field, coef, listed, parts, sides):
    _, modes, times = field.shape
    steps = times // parts
    width = parts * modes
    fine = steps // FT
    half = jnp.bfloat16
    return pl.pallas_call(
        functools.partial(whole_kernel, parts, sides),
        out_shape=jax.ShapeDtypeStruct((sides, parts, fine, 2, modes, FT), half),
        in_specs=[pl.BlockSpec(memory_space=VMEM)] * 9,
        out_specs=pl.BlockSpec(memory_space=VMEM),
        scratch_shapes=[
            VMEM((parts, 2, modes, steps), half),
            VMEM((parts,) + coef.shape, half),
            VMEM((parts,) + listed.shape, jnp.int32),
            pltpu.SMEM((parts,) + listed.shape, jnp.int32),
            VMEM((2, width // MB, MB, steps), jnp.float32),
            VMEM((2, parts * MB, steps), jnp.float32),
            VMEM((2 * width * fine, FT), jnp.float32),
            VMEM((parts, modes, 2 * fine, FT), half),
            VMEM((parts, modes, 2 * fine, FT), half),
            VMEM((parts, fine, 2, modes, FT), half),
            pltpu.SemaphoreType.DMA((7, parts)),
            pltpu.SemaphoreType.DMA((7, parts)),
            pltpu.SemaphoreType.DMA((7,)),
        ],
        compiler_params=pltpu.CompilerParams(
            collective_id=0, has_side_effects=True, vmem_limit_bytes=BIG
        ),
    )(field, coef, listed, *dft_tables(parts))


def dft_tables(parts):
    a = np.arange(FT)
    four = np.exp(-2j * np.pi / FT * (np.outer(a, a) % FT))
    twist = np.exp(-2j * np.pi / NT * (np.outer(a, a) % NT)) / FT
    real = np.block([[four.real, -four.imag], [four.imag, four.real]])
    first = real.reshape(2 * FT, 2, parts, FT // parts).transpose(0, 2, 1, 3)
    first = first.reshape(2 * FT, 2 * FT)
    second = real.reshape(2, FT, 2 * FT).transpose(1, 0, 2).reshape(2 * FT, 2 * FT)

    def split(t):
        t = t.astype(np.float32)
        high = t.astype(jnp.bfloat16)
        return high, (t - high.astype(np.float32)).astype(jnp.bfloat16)

    return (
        *split(first),
        twist.real.astype(np.float32),
        twist.imag.astype(np.float32),
        *split(second),
    )


def dft_kernel(x_ref, f1h, f1l, tw_re, tw_im, f2h, f2l, rows):
    modes = x_ref.shape[1]
    nt = (((1,), (1,)), ((), ()))
    dot = functools.partial(jnp.dot, preferred_element_type=jnp.float32)
    dot_nt = functools.partial(
        lax.dot_general, dimension_numbers=nt, preferred_element_type=jnp.float32
    )
    for m in range(0, modes, 2):
        x = jnp.concatenate(
            [x_ref[:, m].reshape(2 * FT, FT), x_ref[:, m + 1].reshape(2 * FT, FT)], axis=1
        )
        half = dot(f1h[...], x) + dot(f1l[...], x)
        turned = []
        for i in range(2):
            h_re, h_im = half[:FT, i * FT : (i + 1) * FT], half[FT:, i * FT : (i + 1) * FT]
            turned.append(
                jnp.concatenate(
                    [
                        h_re * tw_re[...] - h_im * tw_im[...],
                        h_re * tw_im[...] + h_im * tw_re[...],
                    ],
                    axis=1,
                )
            )
        turned = jnp.concatenate(turned, axis=0)
        high = turned.astype(jnp.bfloat16)
        low = (turned - high.astype(jnp.float32)).astype(jnp.bfloat16)
        out = dot_nt(f2h[...], high) + dot_nt(f2h[...], low) + dot_nt(f2l[...], high)
        for i in range(2):
            rows[pl.ds(m + i, 2 * FT, stride=modes), :] = out[:, i * FT : (i + 1) * FT]


def gram_kernel(scale, half_ref, spec_ref, out_ref):
    sides, parts, _, _, modes, _ = spec_ref.shape
    row_count = out_ref.shape[2]
    sources = row_count // modes
    first = half_ref[0] * sources
    cols, rows_re, rows_im = [], [], []
    for side in range(sides):
        re, im = (spec_ref[side, :, 0, c].reshape(parts * modes, FT) for c in range(2))
        own = pl.ds(first, sources)
        own_re, own_im = (spec_ref[side, own, 0, c].reshape(row_count, FT) for c in range(2))
        cols += [re, im]
        rows_re += [own_re, own_im]
        rows_im += [own_im, -own_re]
    cols = jnp.concatenate(cols, axis=1)
    rows = jnp.concatenate(
        [jnp.concatenate(rows_re, axis=1), jnp.concatenate(rows_im, axis=1)], axis=0
    )
    lane = lax.broadcasted_iota(jnp.int32, rows.shape, 1)
    band = (lane % FT) // FB
    for g in range(FT // FB):
        kept = jnp.where(band == g, rows, jnp.zeros_like(rows))
        out = lax.dot_general(
            kept, cols, (((1,), (1,)), ((), ())), preferred_element_type=jnp.float32
        )
        out_ref[g] = (out * scale).reshape(2, row_count, parts * modes)


def gram(half, spectra, row_count, scale):
    sides, parts, high, _, modes, _ = spectra.shape
    width = parts * modes
    per = FT // FB
    return pl.pallas_call(
        functools.partial(gram_kernel, scale),
        grid=(high,),
        out_shape=jax.ShapeDtypeStruct((high * per, 2, row_count, width), jnp.float32),
        in_specs=[
            pl.BlockSpec(memory_space=pltpu.SMEM),
            pl.BlockSpec((sides, parts, 1, 2, modes, FT), lambda j: (0, 0, j, 0, 0, 0)),
        ],
        out_specs=pl.BlockSpec((per, 2, row_count, width), lambda j: (j, 0, 0, 0)),
        compiler_params=pltpu.CompilerParams(vmem_limit_bytes=BIG),
    )(half, spectra)


def tiled_shards(input_field, kerr_coeff, block_list):
    parts, sides = lax.axis_size("mode"), lax.axis_size("real")
    _, _, modes, times = input_field.shape
    width = parts * modes
    coef = kerr_coeff[0].reshape(MB, MB, MB * MB).transpose(1, 0, 2).reshape(MB * MB, MB * MB)
    listed = jnp.pad(block_list, ((0, 7), (0, FT - block_list.shape[1])))
    spectra = spectra_of(input_field.reshape(2, modes, times), coef, listed, parts, sides)
    half = lax.axis_index("real").astype(jnp.int32).reshape(1)
    return gram(half, spectra, width // sides, 1.0 / (FB * sides))


def tiles_fit(mesh):
    parts = mesh.shape["mode"]
    return FT % parts == 0 and (2 * FT // parts) % 16 == 0 and mesh.shape["real"] <= 2


def either(mesh, input_field, kerr_coeff, block_list):
    modes = input_field.shape[2]
    blocks_each = kerr_coeff.shape[0]
    fits = tiles_fit(mesh) and modes % 16 == 0 and blocks_each == 1
    fits = fits and input_field.shape[1] == 1 and input_field.shape[3] == NT
    return (tiled_shards if fits else shards)(input_field, kerr_coeff, block_list)


def solution(mesh):
    return jax.shard_map(
        functools.partial(either, mesh),
        mesh=mesh,
        in_specs=(P(None, "real", "mode", None), P("mode", None, None), P("mode", None)),
        out_specs=P("mode", None, "real", None),
        check_vma=False,
    )
```

```python
import functools
import math

import jax
import jax.numpy as jnp
import numpy as np
from jax import lax
from jax.experimental import pallas as pl
from jax.experimental.pallas import tpu as pltpu
from jax.sharding import PartitionSpec as P

MB = 8
FT = 128
NT = 16384
FB = 32


kerr_strength = 0.25


def kerr_terms(field_blocks, coeff_group, block_group):
    mode_l = jnp.take(field_blocks, block_group[:, 1], axis=2).astype(jnp.float32)
    mode_m = jnp.take(field_blocks, block_group[:, 2], axis=2).astype(jnp.float32)
    mode_n = jnp.take(field_blocks, block_group[:, 3], axis=2).astype(jnp.float32)
    realiz = field_blocks.shape[1]
    group_size = block_group.shape[0]
    steps_local = field_blocks.shape[4]
    prod_re = (
        mode_m[0][:, :, :, None, :] * mode_n[0][:, :, None, :, :]
        + mode_m[1][:, :, :, None, :] * mode_n[1][:, :, None, :, :]
    )
    prod_im = (
        mode_m[1][:, :, :, None, :] * mode_n[0][:, :, None, :, :]
        - mode_m[0][:, :, :, None, :] * mode_n[1][:, :, None, :, :]
    )
    pairs = (
        jnp.stack([prod_re, prod_im])
        .reshape(2, realiz, group_size, MB * MB, steps_local)
        .astype(jnp.bfloat16)
    )
    weighted = jnp.einsum(
        "kab,crkbt->crkat", coeff_group, pairs, preferred_element_type=jnp.float32
    )
    weighted = weighted.reshape(2, realiz, group_size, MB, MB, steps_local)
    term_re = jnp.sum(
        weighted[0] * mode_l[0][:, :, None] - weighted[1] * mode_l[1][:, :, None], axis=3
    )
    term_im = jnp.sum(
        weighted[0] * mode_l[1][:, :, None] + weighted[1] * mode_l[0][:, :, None], axis=3
    )
    one_hot = (
        block_group[:, 0][:, None] == jnp.arange(field_blocks.shape[2], dtype=jnp.int32)[None, :]
    ).astype(jnp.float32)
    return jnp.einsum(
        "kg,crkpt->crgpt", one_hot, jnp.stack([term_re, term_im]), precision=lax.Precision.HIGHEST
    )


def phase_table(extent, modulus):
    index_a = jnp.arange(extent, dtype=jnp.int32)[:, None]
    index_b = jnp.arange(extent, dtype=jnp.int32)[None, :]
    angle = 2.0 * math.pi / modulus * (index_a * index_b % modulus).astype(jnp.float32)
    return (jnp.cos(angle), -jnp.sin(angle))


def first_pass(table, data):
    table_high = table.astype(jnp.bfloat16)
    table_low = (table - table_high.astype(jnp.float32)).astype(jnp.bfloat16)
    upper = jnp.einsum("kn,rmnj->rmkj", table_high, data, preferred_element_type=jnp.float32)
    return upper + jnp.einsum("kn,rmnj->rmkj", table_low, data, preferred_element_type=jnp.float32)


def second_pass(table, data):
    return jnp.einsum("jn,rmkn->rmjk", table, data, precision=lax.Precision.HIGH)


def transform(by_mode):
    realiz = by_mode.shape[1]
    local_modes = by_mode.shape[2]
    signal = by_mode.reshape(2, realiz, local_modes, FT, FT)
    four_re, four_im = phase_table(FT, FT)
    twist_re, twist_im = phase_table(FT, NT)
    half_re = first_pass(four_re, signal[0]) - first_pass(four_im, signal[1])
    half_im = first_pass(four_re, signal[1]) + first_pass(four_im, signal[0])
    turned_re = half_re * twist_re - half_im * twist_im
    turned_im = half_re * twist_im + half_im * twist_re
    out_re = (second_pass(four_re, turned_re) - second_pass(four_im, turned_im)) / FT
    out_im = (second_pass(four_re, turned_im) + second_pass(four_im, turned_re)) / FT
    return jnp.stack([out_re, out_im]).astype(jnp.bfloat16)


def gram_parts(rows_part, cols_part):
    quarters = jnp.einsum(
        "crpbf,drqbf->bcdpq", rows_part, cols_part, preferred_element_type=jnp.float32
    )
    return jnp.stack(
        [quarters[:, 0, 0] + quarters[:, 1, 1], quarters[:, 1, 0] - quarters[:, 0, 1]], axis=1
    )


def shards(input_field, kerr_coeff, block_list):
    timed = lax.all_to_all(input_field, "mode", split_axis=3, concat_axis=2, tiled=True)
    realiz = timed.shape[1]
    width = timed.shape[2]
    steps_local = timed.shape[3]
    field_blocks = timed.reshape(2, realiz, width // MB, MB, steps_local)
    initial = jnp.zeros(field_blocks.shape, jnp.float32)
    running = initial
    coeff_piece = lax.all_gather(kerr_coeff, "mode", axis=0, tiled=True)
    block_piece = lax.all_gather(block_list, "mode", axis=0, tiled=True)
    block_count = block_piece.shape[0]
    coeff_groups = coeff_piece.reshape(
        block_count // 8, 8, coeff_piece.shape[1], coeff_piece.shape[2]
    )
    block_groups = block_piece.reshape(block_count // 8, 8, 4)

    def one_group(carried, groups):
        return (carried + kerr_terms(field_blocks, groups[0], groups[1]), None)

    running, unused = lax.scan(one_group, running, (coeff_groups, block_groups))
    kerr_sum = running
    kerr_sum = kerr_sum.reshape(2, realiz, width, steps_local)
    base = timed.astype(jnp.float32)
    stepped = jnp.stack(
        [base[0] - kerr_strength * kerr_sum[1], base[1] + kerr_strength * kerr_sum[0]]
    ).astype(jnp.bfloat16)
    by_mode = lax.all_to_all(stepped, "mode", split_axis=2, concat_axis=3, tiled=True)
    spectrum = transform(by_mode)
    banded = lax.all_to_all(spectrum, "mode", split_axis=3, concat_axis=2, tiled=True)
    bands_dev = banded.shape[3] * FT // FB
    spec_bands = banded.reshape(2, realiz, width, bands_dev, FB)
    scale = 1.0 / (FB * realiz * lax.axis_size("real"))
    row_count = width // lax.axis_size("real")
    row_first = lax.axis_index("real") * row_count
    shard_piece = lax.all_gather(spec_bands, "real", axis=1, tiled=True)
    own_part = lax.dynamic_slice_in_dim(shard_piece, row_first, row_count, 2)
    return gram_parts(own_part, shard_piece) * scale


VMEM = pltpu.VMEM
BIG = 60 * 1024 * 1024


def step_order(parts):
    return sorted(range(1, parts), key=lambda step: (-min(step, parts - step), step))


def remote(here, there, sent, landed, target):
    copy = pltpu.make_async_remote_copy(
        src_ref=here,
        dst_ref=there,
        send_sem=sent,
        recv_sem=landed,
        device_id=target,
        device_id_type=pl.DeviceIdType.MESH,
    )
    copy.start()
    return copy


def kerr_terms_at(first, piece, k, list_s, coef, fld, terms):
    span = pl.ds(first, piece)
    bl, bm, bn = (list_s[k, 0, i] for i in (1, 2, 3))
    m_re, m_im = fld[0, bm, :, span][:, None], fld[1, bm, :, span][:, None]
    n_re, n_im = fld[0, bn, :, span][None], fld[1, bn, :, span][None]
    p_re = (m_re * n_re + m_im * n_im).reshape(MB * MB, piece)
    p_im = (m_im * n_re - m_re * n_im).reshape(MB * MB, piece)
    pairs = jnp.concatenate([p_re, p_im], axis=1).astype(jnp.bfloat16)
    w = jnp.dot(coef, pairs, preferred_element_type=jnp.float32)
    w_re = w[:, :piece].reshape(MB, MB, piece)
    w_im = w[:, piece:].reshape(MB, MB, piece)
    l_re, l_im = fld[0, bl, :, span][:, None], fld[1, bl, :, span][:, None]
    at = pl.ds(pl.multiple_of(k * MB, MB), MB)
    terms[0, at, span] = jnp.sum(w_re * l_re - w_im * l_im, axis=0)
    terms[1, at, span] = jnp.sum(w_re * l_im + w_im * l_re, axis=0)


def owner_table(blocks, width, list_s):
    shape = (width, blocks * MB)
    row = lax.broadcasted_iota(jnp.int32, shape, 0)
    col = lax.broadcasted_iota(jnp.int32, shape, 1)
    wanted = jnp.full(shape, -1, jnp.int32)
    for k in range(blocks):
        wanted = jnp.where(col // MB == k, list_s[k, 0, 0] * MB + col % MB, wanted)
    return (row == wanted).astype(jnp.float32).astype(jnp.bfloat16)


def whole_kernel(parts, sides, x_ref, coef_ref, list_ref, f1h, f1l, tw_re, tw_im, f2h, f2l,
                 out_ref, timed, coefs, swapped, lists, list_s, fld, terms, rows, stepped, by_mode, spec,
                 sends, recvs, own_sems):
    me = lax.axis_index("mode")
    other = {"real": 1 - lax.axis_index("real")}
    _, modes, times = x_ref.shape
    steps = times // parts
    width = parts * modes
    groups = width // MB
    fine = steps // FT
    pieces = min(4, fine)
    half = steps // pieces
    piece = min(half, 256)
    order = step_order(parts)
    barrier = pltpu.get_barrier_semaphore()
    for step in order:
        to = {"mode": lax.rem(me + step, parts)}
        pl.semaphore_signal(barrier, inc=1, device_id=to, device_id_type=pl.DeviceIdType.MESH)
    if sides > 1:
        pl.semaphore_signal(barrier, inc=1, device_id=other, device_id_type=pl.DeviceIdType.MESH)
    pl.semaphore_wait(barrier, parts - 1 + (sides > 1))

    def chunk(to, part):
        at = pl.multiple_of(to * steps + part * half, 128)
        return x_ref.at[:, :, pl.ds(at, half)]

    def landing(part):
        return timed.at[me, :, :, pl.ds(part * half, half)]

    small, field_copies = [], [[] for _ in range(pieces)]
    for step in order:
        to = lax.rem(me + step, parts)
        there = {"mode": to}
        small.append(remote(coef_ref, coefs.at[me], sends.at[0, step], recvs.at[0, step], there))
        small.append(remote(list_ref, lists.at[me], sends.at[1, step], recvs.at[1, step], there))
    for part, copies in enumerate(field_copies):
        for step in order:
            to = lax.rem(me + step, parts)
            copies.append(
                remote(
                    chunk(to, part),
                    landing(part),
                    sends.at[4 + part, step],
                    recvs.at[4 + part, step],
                    {"mode": to},
                )
            )
    for slot, (here, there) in enumerate(((coef_ref, coefs.at[me]), (list_ref, lists.at[me]))):
        copy = pltpu.make_async_copy(here, there, own_sems.at[slot])
        copy.start()
        small.append(copy)
    for part, copies in enumerate(field_copies):
        copy = pltpu.make_async_copy(chunk(me, part), landing(part), own_sems.at[4 + part])
        copy.start()
        copies.append(copy)
    for copy in small:
        copy.wait()
    copy = pltpu.make_async_copy(lists, list_s, own_sems.at[2])
    copy.start()
    copy.wait()
    blocks = coefs.shape[0]
    owners = owner_table(blocks, width, list_s)
    order_of = (MB * MB, MB * MB)
    row = lax.broadcasted_iota(jnp.int32, order_of, 0)
    col = lax.broadcasted_iota(jnp.int32, order_of, 1)
    swap = (col == (row % MB) * MB + row // MB).astype(jnp.float32).astype(jnp.bfloat16)
    for k in range(blocks):
        swapped[k] = jnp.dot(
            swap, coefs[k], preferred_element_type=jnp.float32
        ).astype(jnp.bfloat16)
    for part, copies in enumerate(field_copies):
        for copy in copies:
            copy.wait()
        span = pl.ds(part * half, half)
        for c in range(2):
            fld[c, :, :, span] = timed[:, c, :, span].astype(jnp.float32).reshape(groups, MB, half)

        def one_block(k, carry):
            coef = swapped[k]
            for at in range(part * half, (part + 1) * half, piece):
                kerr_terms_at(at, piece, k, list_s, coef, fld, terms)
            return carry

        lax.fori_loop(0, blocks, one_block, 0)
        for c in range(2):
            term = terms[1 - c, :, span]
            high = term.astype(jnp.bfloat16)
            low = (term - high.astype(jnp.float32)).astype(jnp.bfloat16)
            kerr = jnp.dot(owners, high, preferred_element_type=jnp.float32)
            kerr = kerr + jnp.dot(owners, low, preferred_element_type=jnp.float32)
            turn = kerr_strength * (2 * c - 1)
            new = fld[c, :, :, span].reshape(width, half) + turn * kerr
            for g in range(groups):
                for n in range(half // FT):
                    row = g * (MB * 2 * fine) + c * fine + part * (half // FT) + n
                    rows[pl.ds(row, MB, stride=2 * fine), :] = new[
                        g * MB : (g + 1) * MB, n * FT : (n + 1) * FT
                    ]
    stepped[...] = rows[...].astype(jnp.bfloat16).reshape(stepped.shape)

    quarters = min(4, modes // 2)
    few = modes // quarters
    mode_copies = []
    for part in range(quarters):
        some = pl.ds(part * few, few)
        copies = []
        for step in order:
            to = lax.rem(me + step, parts)
            copies.append(
                remote(
                    stepped.at[to, some],
                    by_mode.at[me, some],
                    sends.at[8 + part, step],
                    recvs.at[8 + part, step],
                    {"mode": to},
                )
            )
        copy = pltpu.make_async_copy(
            stepped.at[me, some], by_mode.at[me, some], own_sems.at[8 + part]
        )
        copy.start()
        mode_copies.append(copies + [copy])
    for part, copies in enumerate(mode_copies):
        for copy in copies:
            copy.wait()
        some = range(part * few, (part + 1) * few)
        dft_modes(some, by_mode, f1h, f1l, tw_re, tw_im, f2h, f2l, rows)
    spec[...] = rows[...].astype(jnp.bfloat16).reshape(spec.shape)

    pending, passed = [], []
    for step in order:
        to = lax.rem(me + step, parts)
        pending.append(
            (
                remote(spec.at[to], out_ref.at[0, me], sends.at[2, step], recvs.at[2, step], {"mode": to}),
                lax.rem(me - step + parts, parts),
            )
        )
    copy = pltpu.make_async_copy(spec.at[me], out_ref.at[0, me], own_sems.at[3])
    copy.start()
    if sides > 1:
        passed.append(remote(spec.at[me], out_ref.at[1, me], sends.at[3, 0], recvs.at[3, 0], other))
    for step, (arrival, source) in zip(order, pending):
        arrival.wait_recv()
        if sides > 1:
            passed.append(
                remote(
                    out_ref.at[0, source],
                    out_ref.at[1, source],
                    sends.at[3, step],
                    recvs.at[3, step],
                    other,
                )
            )
    copy.wait()
    for arrival, _ in pending:
        arrival.wait_send()
    for copy in passed:
        copy.wait()


def spectra_of(field, coef, listed, parts, sides):
    _, modes, times = field.shape
    steps = times // parts
    width = parts * modes
    fine = steps // FT
    half = jnp.bfloat16
    return pl.pallas_call(
        functools.partial(whole_kernel, parts, sides),
        out_shape=jax.ShapeDtypeStruct((sides, parts, fine, 2, modes, FT), half),
        in_specs=[pl.BlockSpec(memory_space=pl.ANY)] + [pl.BlockSpec(memory_space=VMEM)] * 8,
        out_specs=pl.BlockSpec(memory_space=VMEM),
        scratch_shapes=[
            VMEM((parts, 2, modes, steps), half),
            VMEM((parts,) + coef.shape, half),
            VMEM((parts,) + coef.shape, half),
            VMEM((parts,) + listed.shape, jnp.int32),
            pltpu.SMEM((parts,) + listed.shape, jnp.int32),
            VMEM((2, width // MB, MB, steps), jnp.float32),
            VMEM((2, parts * MB, steps), jnp.float32),
            VMEM((2 * width * fine, FT), jnp.float32),
            VMEM((parts, modes, 2 * fine, FT), half),
            VMEM((parts, modes, 2 * fine, FT), half),
            VMEM((parts, fine, 2, modes, FT), half),
            pltpu.SemaphoreType.DMA((12, parts)),
            pltpu.SemaphoreType.DMA((12, parts)),
            pltpu.SemaphoreType.DMA((12,)),
        ],
        compiler_params=pltpu.CompilerParams(
            collective_id=0, has_side_effects=True, vmem_limit_bytes=BIG
        ),
    )(field, coef, listed, *dft_tables(parts))


def dft_tables(parts):
    a = np.arange(FT)
    four = np.exp(-2j * np.pi / FT * (np.outer(a, a) % FT))
    twist = np.exp(-2j * np.pi / NT * (np.outer(a, a) % NT)) / FT
    real = np.block([[four.real, -four.imag], [four.imag, four.real]])
    first = real.reshape(2 * FT, 2, parts, FT // parts).transpose(0, 2, 1, 3)
    first = first.reshape(2 * FT, 2 * FT)
    second = real.reshape(2, FT, 2 * FT).transpose(1, 0, 2).reshape(2 * FT, 2 * FT)

    def split(t):
        t = t.astype(np.float32)
        high = t.astype(jnp.bfloat16)
        return high, (t - high.astype(np.float32)).astype(jnp.bfloat16)

    return (
        *split(first),
        twist.real.astype(np.float32),
        twist.imag.astype(np.float32),
        *split(second),
    )


def dft_modes(some, x_ref, f1h, f1l, tw_re, tw_im, f2h, f2l, rows):
    modes = x_ref.shape[1]
    nt = (((1,), (1,)), ((), ()))
    dot = functools.partial(jnp.dot, preferred_element_type=jnp.float32)
    dot_nt = functools.partial(
        lax.dot_general, dimension_numbers=nt, preferred_element_type=jnp.float32
    )
    for m in some[::2]:
        x = jnp.concatenate(
            [x_ref[:, m].reshape(2 * FT, FT), x_ref[:, m + 1].reshape(2 * FT, FT)], axis=1
        )
        half = dot(f1h[...], x) + dot(f1l[...], x)
        turned = []
        for i in range(2):
            h_re, h_im = half[:FT, i * FT : (i + 1) * FT], half[FT:, i * FT : (i + 1) * FT]
            turned.append(
                jnp.concatenate(
                    [
                        h_re * tw_re[...] - h_im * tw_im[...],
                        h_re * tw_im[...] + h_im * tw_re[...],
                    ],
                    axis=1,
                )
            )
        turned = jnp.concatenate(turned, axis=0)
        high = turned.astype(jnp.bfloat16)
        low = (turned - high.astype(jnp.float32)).astype(jnp.bfloat16)
        out = dot_nt(f2h[...], high) + dot_nt(f2h[...], low) + dot_nt(f2l[...], high)
        for i in range(2):
            rows[pl.ds(m + i, 2 * FT, stride=modes), :] = out[:, i * FT : (i + 1) * FT]


def gram_kernel(scale, half_ref, spec_ref, out_ref):
    sides, parts, _, _, modes, _ = spec_ref.shape
    row_count = out_ref.shape[2]
    sources = row_count // modes
    first = half_ref[0] * sources
    cols, rows_re, rows_im = [], [], []
    for side in range(sides):
        re, im = (spec_ref[side, :, 0, c].reshape(parts * modes, FT) for c in range(2))
        own = pl.ds(first, sources)
        own_re, own_im = (spec_ref[side, own, 0, c].reshape(row_count, FT) for c in range(2))
        cols += [re, im]
        rows_re += [own_re, own_im]
        rows_im += [own_im, -own_re]
    cols = jnp.concatenate(cols, axis=1)
    rows = jnp.concatenate(
        [jnp.concatenate(rows_re, axis=1), jnp.concatenate(rows_im, axis=1)], axis=0
    )
    lane = lax.broadcasted_iota(jnp.int32, rows.shape, 1)
    band = (lane % FT) // FB
    for g in range(FT // FB):
        kept = jnp.where(band == g, rows, jnp.zeros_like(rows))
        out = lax.dot_general(
            kept, cols, (((1,), (1,)), ((), ())), preferred_element_type=jnp.float32
        )
        out_ref[g] = (out * scale).reshape(2, row_count, parts * modes)


def gram(half, spectra, row_count, scale):
    sides, parts, high, _, modes, _ = spectra.shape
    width = parts * modes
    per = FT // FB
    return pl.pallas_call(
        functools.partial(gram_kernel, scale),
        grid=(high,),
        out_shape=jax.ShapeDtypeStruct((high * per, 2, row_count, width), jnp.float32),
        in_specs=[
            pl.BlockSpec(memory_space=pltpu.SMEM),
            pl.BlockSpec((sides, parts, 1, 2, modes, FT), lambda j: (0, 0, j, 0, 0, 0)),
        ],
        out_specs=pl.BlockSpec((per, 2, row_count, width), lambda j: (j, 0, 0, 0)),
        compiler_params=pltpu.CompilerParams(vmem_limit_bytes=BIG),
    )(half, spectra)


def tiled_shards(input_field, kerr_coeff, block_list):
    parts, sides = lax.axis_size("mode"), lax.axis_size("real")
    _, _, modes, times = input_field.shape
    width = parts * modes
    spectra = spectra_of(
        input_field.reshape(2, modes, times), kerr_coeff[0], block_list, parts, sides
    )
    half = lax.axis_index("real").astype(jnp.int32).reshape(1)
    return gram(half, spectra, width // sides, 1.0 / (FB * sides))


def tiles_fit(mesh):
    parts = mesh.shape["mode"]
    return FT % parts == 0 and (2 * FT // parts) % 16 == 0 and mesh.shape["real"] <= 2


def either(mesh, input_field, kerr_coeff, block_list):
    modes = input_field.shape[2]
    blocks_each = kerr_coeff.shape[0]
    fits = tiles_fit(mesh) and modes % 16 == 0 and blocks_each == 1
    fits = fits and input_field.shape[1] == 1 and input_field.shape[3] == NT
    return (tiled_shards if fits else shards)(input_field, kerr_coeff, block_list)


def solution(mesh):
    return jax.shard_map(
        functools.partial(either, mesh),
        mesh=mesh,
        in_specs=(P(None, "real", "mode", None), P("mode", None, None), P("mode", None)),
        out_specs=P("mode", None, "real", None),
        check_vma=False,
    )
```

```python
import functools
import math

import jax
import jax.numpy as jnp
import numpy as np
from jax import lax
from jax.experimental import pallas as pl
from jax.experimental.pallas import tpu as pltpu
from jax.sharding import PartitionSpec as P

MB = 8
FT = 128
NT = 16384
FB = 32


kerr_strength = 0.25


def kerr_terms(field_blocks, coeff_group, block_group):
    mode_l = jnp.take(field_blocks, block_group[:, 1], axis=2).astype(jnp.float32)
    mode_m = jnp.take(field_blocks, block_group[:, 2], axis=2).astype(jnp.float32)
    mode_n = jnp.take(field_blocks, block_group[:, 3], axis=2).astype(jnp.float32)
    realiz = field_blocks.shape[1]
    group_size = block_group.shape[0]
    steps_local = field_blocks.shape[4]
    prod_re = (
        mode_m[0][:, :, :, None, :] * mode_n[0][:, :, None, :, :]
        + mode_m[1][:, :, :, None, :] * mode_n[1][:, :, None, :, :]
    )
    prod_im = (
        mode_m[1][:, :, :, None, :] * mode_n[0][:, :, None, :, :]
        - mode_m[0][:, :, :, None, :] * mode_n[1][:, :, None, :, :]
    )
    pairs = (
        jnp.stack([prod_re, prod_im])
        .reshape(2, realiz, group_size, MB * MB, steps_local)
        .astype(jnp.bfloat16)
    )
    weighted = jnp.einsum(
        "kab,crkbt->crkat", coeff_group, pairs, preferred_element_type=jnp.float32
    )
    weighted = weighted.reshape(2, realiz, group_size, MB, MB, steps_local)
    term_re = jnp.sum(
        weighted[0] * mode_l[0][:, :, None] - weighted[1] * mode_l[1][:, :, None], axis=3
    )
    term_im = jnp.sum(
        weighted[0] * mode_l[1][:, :, None] + weighted[1] * mode_l[0][:, :, None], axis=3
    )
    one_hot = (
        block_group[:, 0][:, None] == jnp.arange(field_blocks.shape[2], dtype=jnp.int32)[None, :]
    ).astype(jnp.float32)
    return jnp.einsum(
        "kg,crkpt->crgpt", one_hot, jnp.stack([term_re, term_im]), precision=lax.Precision.HIGHEST
    )


def phase_table(extent, modulus):
    index_a = jnp.arange(extent, dtype=jnp.int32)[:, None]
    index_b = jnp.arange(extent, dtype=jnp.int32)[None, :]
    angle = 2.0 * math.pi / modulus * (index_a * index_b % modulus).astype(jnp.float32)
    return (jnp.cos(angle), -jnp.sin(angle))


def first_pass(table, data):
    table_high = table.astype(jnp.bfloat16)
    table_low = (table - table_high.astype(jnp.float32)).astype(jnp.bfloat16)
    upper = jnp.einsum("kn,rmnj->rmkj", table_high, data, preferred_element_type=jnp.float32)
    return upper + jnp.einsum("kn,rmnj->rmkj", table_low, data, preferred_element_type=jnp.float32)


def second_pass(table, data):
    return jnp.einsum("jn,rmkn->rmjk", table, data, precision=lax.Precision.HIGH)


def transform(by_mode):
    realiz = by_mode.shape[1]
    local_modes = by_mode.shape[2]
    signal = by_mode.reshape(2, realiz, local_modes, FT, FT)
    four_re, four_im = phase_table(FT, FT)
    twist_re, twist_im = phase_table(FT, NT)
    half_re = first_pass(four_re, signal[0]) - first_pass(four_im, signal[1])
    half_im = first_pass(four_re, signal[1]) + first_pass(four_im, signal[0])
    turned_re = half_re * twist_re - half_im * twist_im
    turned_im = half_re * twist_im + half_im * twist_re
    out_re = (second_pass(four_re, turned_re) - second_pass(four_im, turned_im)) / FT
    out_im = (second_pass(four_re, turned_im) + second_pass(four_im, turned_re)) / FT
    return jnp.stack([out_re, out_im]).astype(jnp.bfloat16)


def gram_parts(rows_part, cols_part):
    mode_parts = jnp.einsum(
        "crpbf,drqbf->bcdpq", rows_part, cols_part, preferred_element_type=jnp.float32
    )
    return jnp.stack(
        [mode_parts[:, 0, 0] + mode_parts[:, 1, 1], mode_parts[:, 1, 0] - mode_parts[:, 0, 1]], axis=1
    )


def shards(input_field, kerr_coeff, block_list):
    timed = lax.all_to_all(input_field, "mode", split_axis=3, concat_axis=2, tiled=True)
    realiz = timed.shape[1]
    width = timed.shape[2]
    steps_local = timed.shape[3]
    field_blocks = timed.reshape(2, realiz, width // MB, MB, steps_local)
    initial = jnp.zeros(field_blocks.shape, jnp.float32)
    running = initial
    coeff_piece = lax.all_gather(kerr_coeff, "mode", axis=0, tiled=True)
    block_piece = lax.all_gather(block_list, "mode", axis=0, tiled=True)
    block_count = block_piece.shape[0]
    coeff_groups = coeff_piece.reshape(
        block_count // 8, 8, coeff_piece.shape[1], coeff_piece.shape[2]
    )
    block_groups = block_piece.reshape(block_count // 8, 8, 4)

    def one_group(carried, groups):
        return (carried + kerr_terms(field_blocks, groups[0], groups[1]), None)

    running, unused = lax.scan(one_group, running, (coeff_groups, block_groups))
    kerr_sum = running
    kerr_sum = kerr_sum.reshape(2, realiz, width, steps_local)
    base = timed.astype(jnp.float32)
    stepped = jnp.stack(
        [base[0] - kerr_strength * kerr_sum[1], base[1] + kerr_strength * kerr_sum[0]]
    ).astype(jnp.bfloat16)
    by_mode = lax.all_to_all(stepped, "mode", split_axis=2, concat_axis=3, tiled=True)
    spectrum = transform(by_mode)
    banded = lax.all_to_all(spectrum, "mode", split_axis=3, concat_axis=2, tiled=True)
    bands_dev = banded.shape[3] * FT // FB
    spec_bands = banded.reshape(2, realiz, width, bands_dev, FB)
    scale = 1.0 / (FB * realiz * lax.axis_size("real"))
    row_count = width // lax.axis_size("real")
    row_first = lax.axis_index("real") * row_count
    shard_piece = lax.all_gather(spec_bands, "real", axis=1, tiled=True)
    own_part = lax.dynamic_slice_in_dim(shard_piece, row_first, row_count, 2)
    return gram_parts(own_part, shard_piece) * scale


VMEM = pltpu.VMEM
BIG = 60 * 1024 * 1024


def step_order(parts):
    return sorted(range(1, parts), key=lambda step: (-min(step, parts - step), step))


def remote(here, there, sent, landed, target):
    copy = pltpu.make_async_remote_copy(
        src_ref=here,
        dst_ref=there,
        send_sem=sent,
        recv_sem=landed,
        device_id=target,
        device_id_type=pl.DeviceIdType.MESH,
    )
    copy.start()
    return copy


def kerr_terms_at(first, piece, k, list_s, coef, fld, terms):
    span = pl.ds(first, piece)
    bl, bm, bn = (list_s[k, 0, i] for i in (1, 2, 3))
    m_re, m_im = fld[0, bm, :, span][:, None], fld[1, bm, :, span][:, None]
    n_re, n_im = fld[0, bn, :, span][None], fld[1, bn, :, span][None]
    p_re = (m_re * n_re + m_im * n_im).reshape(MB * MB, piece)
    p_im = (m_im * n_re - m_re * n_im).reshape(MB * MB, piece)
    pairs = jnp.concatenate([p_re, p_im], axis=1).astype(jnp.bfloat16)
    w = jnp.dot(coef, pairs, preferred_element_type=jnp.float32)
    w_re = w[:, :piece].reshape(MB, MB, piece)
    w_im = w[:, piece:].reshape(MB, MB, piece)
    l_re, l_im = fld[0, bl, :, span][:, None], fld[1, bl, :, span][:, None]
    at = pl.ds(pl.multiple_of(k * MB, MB), MB)
    terms[0, at, span] = jnp.sum(w_re * l_re - w_im * l_im, axis=0)
    terms[1, at, span] = jnp.sum(w_re * l_im + w_im * l_re, axis=0)


def owner_table(blocks, width, list_s):
    shape = (width, blocks * MB)
    row = lax.broadcasted_iota(jnp.int32, shape, 0)
    col = lax.broadcasted_iota(jnp.int32, shape, 1)
    wanted = jnp.full(shape, -1, jnp.int32)
    for k in range(blocks):
        wanted = jnp.where(col // MB == k, list_s[k, 0, 0] * MB + col % MB, wanted)
    return (row == wanted).astype(jnp.float32).astype(jnp.bfloat16)


def whole_kernel(parts, sides, x_ref, coef_ref, list_ref, f1h, f1l, tw_re, tw_im, f2h, f2l,
                 out_ref, timed, coefs, swapped, lists, list_s, fld, terms, rows, stepped, by_mode, spec,
                 sends, recvs, own_sems):
    me = lax.axis_index("mode")
    other = {"real": 1 - lax.axis_index("real")}
    _, modes, times = x_ref.shape
    steps = times // parts
    width = parts * modes
    groups = width // MB
    fine = steps // FT
    pieces = min(2, fine)
    half = steps // pieces
    piece = min(half, 256)
    order = step_order(parts)
    barrier = pltpu.get_barrier_semaphore()
    for step in order:
        to = {"mode": lax.rem(me + step, parts)}
        pl.semaphore_signal(barrier, inc=1, device_id=to, device_id_type=pl.DeviceIdType.MESH)
    if sides > 1:
        pl.semaphore_signal(barrier, inc=1, device_id=other, device_id_type=pl.DeviceIdType.MESH)
    pl.semaphore_wait(barrier, parts - 1 + (sides > 1))

    def chunk(to, part):
        at = pl.multiple_of(to * steps + part * half, 128)
        return x_ref.at[:, :, pl.ds(at, half)]

    def landing(part):
        return timed.at[me, :, :, pl.ds(part * half, half)]

    small, field_copies = [], [[] for _ in range(pieces)]
    for step in order:
        to = lax.rem(me + step, parts)
        there = {"mode": to}
        small.append(remote(coef_ref, coefs.at[me], sends.at[0, step], recvs.at[0, step], there))
        small.append(remote(list_ref, lists.at[me], sends.at[1, step], recvs.at[1, step], there))
    for part, copies in enumerate(field_copies):
        for step in order:
            to = lax.rem(me + step, parts)
            copies.append(
                remote(
                    chunk(to, part),
                    landing(part),
                    sends.at[4 + part, step],
                    recvs.at[4 + part, step],
                    {"mode": to},
                )
            )
    for slot, (here, there) in enumerate(((coef_ref, coefs.at[me]), (list_ref, lists.at[me]))):
        copy = pltpu.make_async_copy(here, there, own_sems.at[slot])
        copy.start()
        small.append(copy)
    for part, copies in enumerate(field_copies):
        copy = pltpu.make_async_copy(chunk(me, part), landing(part), own_sems.at[4 + part])
        copy.start()
        copies.append(copy)
    for copy in small:
        copy.wait()
    copy = pltpu.make_async_copy(lists, list_s, own_sems.at[2])
    copy.start()
    copy.wait()
    blocks = coefs.shape[0]
    owners = owner_table(blocks, width, list_s)
    order_of = (MB * MB, MB * MB)
    row = lax.broadcasted_iota(jnp.int32, order_of, 0)
    col = lax.broadcasted_iota(jnp.int32, order_of, 1)
    swap = (col == (row % MB) * MB + row // MB).astype(jnp.float32).astype(jnp.bfloat16)
    for k in range(blocks):
        swapped[k] = jnp.dot(
            swap, coefs[k], preferred_element_type=jnp.float32
        ).astype(jnp.bfloat16)
    for part, copies in enumerate(field_copies):
        for copy in copies:
            copy.wait()
        span = pl.ds(part * half, half)
        for c in range(2):
            fld[c, :, :, span] = timed[:, c, :, span].astype(jnp.float32).reshape(groups, MB, half)

        def one_block(k, carry):
            coef = swapped[k]
            for at in range(part * half, (part + 1) * half, piece):
                kerr_terms_at(at, piece, k, list_s, coef, fld, terms)
            return carry

        lax.fori_loop(0, blocks, one_block, 0)
        for c in range(2):
            term = terms[1 - c, :, span]
            high = term.astype(jnp.bfloat16)
            low = (term - high.astype(jnp.float32)).astype(jnp.bfloat16)
            kerr = jnp.dot(owners, high, preferred_element_type=jnp.float32)
            kerr = kerr + jnp.dot(owners, low, preferred_element_type=jnp.float32)
            turn = kerr_strength * (2 * c - 1)
            new = fld[c, :, :, span].reshape(width, half) + turn * kerr
            for g in range(groups):
                for n in range(half // FT):
                    row = g * (MB * 2 * fine) + c * fine + part * (half // FT) + n
                    rows[pl.ds(row, MB, stride=2 * fine), :] = new[
                        g * MB : (g + 1) * MB, n * FT : (n + 1) * FT
                    ]
    stepped[...] = rows[...].astype(jnp.bfloat16).reshape(stepped.shape)

    mode_parts = min(2, modes // 2)
    few = modes // mode_parts
    mode_copies = []
    for part in range(mode_parts):
        some = pl.ds(part * few, few)
        copies = []
        for step in order:
            to = lax.rem(me + step, parts)
            copies.append(
                remote(
                    stepped.at[to, some],
                    by_mode.at[me, some],
                    sends.at[8 + part, step],
                    recvs.at[8 + part, step],
                    {"mode": to},
                )
            )
        copy = pltpu.make_async_copy(
            stepped.at[me, some], by_mode.at[me, some], own_sems.at[8 + part]
        )
        copy.start()
        mode_copies.append(copies + [copy])
    for part, copies in enumerate(mode_copies):
        for copy in copies:
            copy.wait()
        some = range(part * few, (part + 1) * few)
        dft_modes(some, by_mode, f1h, f1l, tw_re, tw_im, f2h, f2l, rows)
    spec[...] = rows[...].astype(jnp.bfloat16).reshape(spec.shape)

    pending, passed = [], []
    for step in order:
        to = lax.rem(me + step, parts)
        pending.append(
            (
                remote(spec.at[to], out_ref.at[0, me], sends.at[2, step], recvs.at[2, step], {"mode": to}),
                lax.rem(me - step + parts, parts),
            )
        )
    copy = pltpu.make_async_copy(spec.at[me], out_ref.at[0, me], own_sems.at[3])
    copy.start()
    if sides > 1:
        passed.append(remote(spec.at[me], out_ref.at[1, me], sends.at[3, 0], recvs.at[3, 0], other))
    for step, (arrival, source) in zip(order, pending):
        arrival.wait_recv()
        if sides > 1:
            passed.append(
                remote(
                    out_ref.at[0, source],
                    out_ref.at[1, source],
                    sends.at[3, step],
                    recvs.at[3, step],
                    other,
                )
            )
    copy.wait()
    for arrival, _ in pending:
        arrival.wait_send()
    for copy in passed:
        copy.wait()


def spectra_of(field, coef, listed, parts, sides):
    _, modes, times = field.shape
    steps = times // parts
    width = parts * modes
    fine = steps // FT
    half = jnp.bfloat16
    return pl.pallas_call(
        functools.partial(whole_kernel, parts, sides),
        out_shape=jax.ShapeDtypeStruct((sides, parts, fine, 2, modes, FT), half),
        in_specs=[pl.BlockSpec(memory_space=pl.ANY)] + [pl.BlockSpec(memory_space=VMEM)] * 8,
        out_specs=pl.BlockSpec(memory_space=VMEM),
        scratch_shapes=[
            VMEM((parts, 2, modes, steps), half),
            VMEM((parts,) + coef.shape, half),
            VMEM((parts,) + coef.shape, half),
            VMEM((parts,) + listed.shape, jnp.int32),
            pltpu.SMEM((parts,) + listed.shape, jnp.int32),
            VMEM((2, width // MB, MB, steps), jnp.float32),
            VMEM((2, parts * MB, steps), jnp.float32),
            VMEM((2 * width * fine, FT), jnp.float32),
            VMEM((parts, modes, 2 * fine, FT), half),
            VMEM((parts, modes, 2 * fine, FT), half),
            VMEM((parts, fine, 2, modes, FT), half),
            pltpu.SemaphoreType.DMA((12, parts)),
            pltpu.SemaphoreType.DMA((12, parts)),
            pltpu.SemaphoreType.DMA((12,)),
        ],
        compiler_params=pltpu.CompilerParams(
            collective_id=0, has_side_effects=True, vmem_limit_bytes=BIG
        ),
    )(field, coef, listed, *dft_tables(parts))


def dft_tables(parts):
    a = np.arange(FT)
    four = np.exp(-2j * np.pi / FT * (np.outer(a, a) % FT))
    twist = np.exp(-2j * np.pi / NT * (np.outer(a, a) % NT)) / FT
    real = np.block([[four.real, -four.imag], [four.imag, four.real]])
    first = real.reshape(2 * FT, 2, parts, FT // parts).transpose(0, 2, 1, 3)
    first = first.reshape(2 * FT, 2 * FT)
    second = real.reshape(2, FT, 2 * FT).transpose(1, 0, 2).reshape(2 * FT, 2 * FT)

    def split(t):
        t = t.astype(np.float32)
        high = t.astype(jnp.bfloat16)
        return high, (t - high.astype(np.float32)).astype(jnp.bfloat16)

    return (
        *split(first),
        twist.real.astype(np.float32),
        twist.imag.astype(np.float32),
        *split(second),
    )


def dft_modes(some, x_ref, f1h, f1l, tw_re, tw_im, f2h, f2l, rows):
    modes = x_ref.shape[1]
    nt = (((1,), (1,)), ((), ()))
    dot = functools.partial(jnp.dot, preferred_element_type=jnp.float32)
    dot_nt = functools.partial(
        lax.dot_general, dimension_numbers=nt, preferred_element_type=jnp.float32
    )
    for m in some[::2]:
        x = jnp.concatenate(
            [x_ref[:, m].reshape(2 * FT, FT), x_ref[:, m + 1].reshape(2 * FT, FT)], axis=1
        )
        half = dot(f1h[...], x) + dot(f1l[...], x)
        turned = []
        for i in range(2):
            h_re, h_im = half[:FT, i * FT : (i + 1) * FT], half[FT:, i * FT : (i + 1) * FT]
            turned.append(
                jnp.concatenate(
                    [
                        h_re * tw_re[...] - h_im * tw_im[...],
                        h_re * tw_im[...] + h_im * tw_re[...],
                    ],
                    axis=1,
                )
            )
        turned = jnp.concatenate(turned, axis=0)
        high = turned.astype(jnp.bfloat16)
        low = (turned - high.astype(jnp.float32)).astype(jnp.bfloat16)
        out = dot_nt(f2h[...], high) + dot_nt(f2h[...], low) + dot_nt(f2l[...], high)
        for i in range(2):
            rows[pl.ds(m + i, 2 * FT, stride=modes), :] = out[:, i * FT : (i + 1) * FT]


def gram_kernel(scale, half_ref, spec_ref, out_ref):
    sides, parts, _, _, modes, _ = spec_ref.shape
    row_count = out_ref.shape[2]
    sources = row_count // modes
    first = half_ref[0] * sources
    cols, rows_re, rows_im = [], [], []
    for side in range(sides):
        re, im = (spec_ref[side, :, 0, c].reshape(parts * modes, FT) for c in range(2))
        own = pl.ds(first, sources)
        own_re, own_im = (spec_ref[side, own, 0, c].reshape(row_count, FT) for c in range(2))
        cols += [re, im]
        rows_re += [own_re, own_im]
        rows_im += [own_im, -own_re]
    cols = jnp.concatenate(cols, axis=1)
    rows = jnp.concatenate(
        [jnp.concatenate(rows_re, axis=1), jnp.concatenate(rows_im, axis=1)], axis=0
    )
    lane = lax.broadcasted_iota(jnp.int32, rows.shape, 1)
    band = (lane % FT) // FB
    for g in range(FT // FB):
        kept = jnp.where(band == g, rows, jnp.zeros_like(rows))
        out = lax.dot_general(
            kept, cols, (((1,), (1,)), ((), ())), preferred_element_type=jnp.float32
        )
        out_ref[g] = (out * scale).reshape(2, row_count, parts * modes)


def gram(half, spectra, row_count, scale):
    sides, parts, high, _, modes, _ = spectra.shape
    width = parts * modes
    per = FT // FB
    return pl.pallas_call(
        functools.partial(gram_kernel, scale),
        grid=(high,),
        out_shape=jax.ShapeDtypeStruct((high * per, 2, row_count, width), jnp.float32),
        in_specs=[
            pl.BlockSpec(memory_space=pltpu.SMEM),
            pl.BlockSpec((sides, parts, 1, 2, modes, FT), lambda j: (0, 0, j, 0, 0, 0)),
        ],
        out_specs=pl.BlockSpec((per, 2, row_count, width), lambda j: (j, 0, 0, 0)),
        compiler_params=pltpu.CompilerParams(vmem_limit_bytes=BIG),
    )(half, spectra)


def tiled_shards(input_field, kerr_coeff, block_list):
    parts, sides = lax.axis_size("mode"), lax.axis_size("real")
    _, _, modes, times = input_field.shape
    width = parts * modes
    spectra = spectra_of(
        input_field.reshape(2, modes, times), kerr_coeff[0], block_list, parts, sides
    )
    half = lax.axis_index("real").astype(jnp.int32).reshape(1)
    return gram(half, spectra, width // sides, 1.0 / (FB * sides))


def tiles_fit(mesh):
    parts = mesh.shape["mode"]
    return FT % parts == 0 and (2 * FT // parts) % 16 == 0 and mesh.shape["real"] <= 2


def either(mesh, input_field, kerr_coeff, block_list):
    modes = input_field.shape[2]
    blocks_each = kerr_coeff.shape[0]
    fits = tiles_fit(mesh) and modes % 16 == 0 and blocks_each == 1
    fits = fits and input_field.shape[1] == 1 and input_field.shape[3] == NT
    return (tiled_shards if fits else shards)(input_field, kerr_coeff, block_list)


def solution(mesh):
    return jax.shard_map(
        functools.partial(either, mesh),
        mesh=mesh,
        in_specs=(P(None, "real", "mode", None), P("mode", None, None), P("mode", None)),
        out_specs=P("mode", None, "real", None),
        check_vma=False,
    )
```

```python
import functools
import math

import jax
import jax.numpy as jnp
import numpy as np
from jax import lax
from jax.experimental import pallas as pl
from jax.experimental.pallas import tpu as pltpu
from jax.sharding import PartitionSpec as P

MB = 8
FT = 128
NT = 16384
FB = 32


kerr_strength = 0.25


def kerr_terms(field_blocks, coeff_group, block_group):
    mode_l = jnp.take(field_blocks, block_group[:, 1], axis=2).astype(jnp.float32)
    mode_m = jnp.take(field_blocks, block_group[:, 2], axis=2).astype(jnp.float32)
    mode_n = jnp.take(field_blocks, block_group[:, 3], axis=2).astype(jnp.float32)
    realiz = field_blocks.shape[1]
    group_size = block_group.shape[0]
    steps_local = field_blocks.shape[4]
    prod_re = (
        mode_m[0][:, :, :, None, :] * mode_n[0][:, :, None, :, :]
        + mode_m[1][:, :, :, None, :] * mode_n[1][:, :, None, :, :]
    )
    prod_im = (
        mode_m[1][:, :, :, None, :] * mode_n[0][:, :, None, :, :]
        - mode_m[0][:, :, :, None, :] * mode_n[1][:, :, None, :, :]
    )
    pairs = (
        jnp.stack([prod_re, prod_im])
        .reshape(2, realiz, group_size, MB * MB, steps_local)
        .astype(jnp.bfloat16)
    )
    weighted = jnp.einsum(
        "kab,crkbt->crkat", coeff_group, pairs, preferred_element_type=jnp.float32
    )
    weighted = weighted.reshape(2, realiz, group_size, MB, MB, steps_local)
    term_re = jnp.sum(
        weighted[0] * mode_l[0][:, :, None] - weighted[1] * mode_l[1][:, :, None], axis=3
    )
    term_im = jnp.sum(
        weighted[0] * mode_l[1][:, :, None] + weighted[1] * mode_l[0][:, :, None], axis=3
    )
    one_hot = (
        block_group[:, 0][:, None] == jnp.arange(field_blocks.shape[2], dtype=jnp.int32)[None, :]
    ).astype(jnp.float32)
    return jnp.einsum(
        "kg,crkpt->crgpt", one_hot, jnp.stack([term_re, term_im]), precision=lax.Precision.HIGHEST
    )


def phase_table(extent, modulus):
    index_a = jnp.arange(extent, dtype=jnp.int32)[:, None]
    index_b = jnp.arange(extent, dtype=jnp.int32)[None, :]
    angle = 2.0 * math.pi / modulus * (index_a * index_b % modulus).astype(jnp.float32)
    return (jnp.cos(angle), -jnp.sin(angle))


def first_pass(table, data):
    table_high = table.astype(jnp.bfloat16)
    table_low = (table - table_high.astype(jnp.float32)).astype(jnp.bfloat16)
    upper = jnp.einsum("kn,rmnj->rmkj", table_high, data, preferred_element_type=jnp.float32)
    return upper + jnp.einsum("kn,rmnj->rmkj", table_low, data, preferred_element_type=jnp.float32)


def second_pass(table, data):
    return jnp.einsum("jn,rmkn->rmjk", table, data, precision=lax.Precision.HIGH)


def transform(by_mode):
    realiz = by_mode.shape[1]
    local_modes = by_mode.shape[2]
    signal = by_mode.reshape(2, realiz, local_modes, FT, FT)
    four_re, four_im = phase_table(FT, FT)
    twist_re, twist_im = phase_table(FT, NT)
    half_re = first_pass(four_re, signal[0]) - first_pass(four_im, signal[1])
    half_im = first_pass(four_re, signal[1]) + first_pass(four_im, signal[0])
    turned_re = half_re * twist_re - half_im * twist_im
    turned_im = half_re * twist_im + half_im * twist_re
    out_re = (second_pass(four_re, turned_re) - second_pass(four_im, turned_im)) / FT
    out_im = (second_pass(four_re, turned_im) + second_pass(four_im, turned_re)) / FT
    return jnp.stack([out_re, out_im]).astype(jnp.bfloat16)


def gram_parts(rows_part, cols_part):
    mode_parts = jnp.einsum(
        "crpbf,drqbf->bcdpq", rows_part, cols_part, preferred_element_type=jnp.float32
    )
    return jnp.stack(
        [mode_parts[:, 0, 0] + mode_parts[:, 1, 1], mode_parts[:, 1, 0] - mode_parts[:, 0, 1]], axis=1
    )


def shards(input_field, kerr_coeff, block_list):
    timed = lax.all_to_all(input_field, "mode", split_axis=3, concat_axis=2, tiled=True)
    realiz = timed.shape[1]
    width = timed.shape[2]
    steps_local = timed.shape[3]
    field_blocks = timed.reshape(2, realiz, width // MB, MB, steps_local)
    initial = jnp.zeros(field_blocks.shape, jnp.float32)
    running = initial
    coeff_piece = lax.all_gather(kerr_coeff, "mode", axis=0, tiled=True)
    block_piece = lax.all_gather(block_list, "mode", axis=0, tiled=True)
    block_count = block_piece.shape[0]
    coeff_groups = coeff_piece.reshape(
        block_count // 8, 8, coeff_piece.shape[1], coeff_piece.shape[2]
    )
    block_groups = block_piece.reshape(block_count // 8, 8, 4)

    def one_group(carried, groups):
        return (carried + kerr_terms(field_blocks, groups[0], groups[1]), None)

    running, unused = lax.scan(one_group, running, (coeff_groups, block_groups))
    kerr_sum = running
    kerr_sum = kerr_sum.reshape(2, realiz, width, steps_local)
    base = timed.astype(jnp.float32)
    stepped = jnp.stack(
        [base[0] - kerr_strength * kerr_sum[1], base[1] + kerr_strength * kerr_sum[0]]
    ).astype(jnp.bfloat16)
    by_mode = lax.all_to_all(stepped, "mode", split_axis=2, concat_axis=3, tiled=True)
    spectrum = transform(by_mode)
    banded = lax.all_to_all(spectrum, "mode", split_axis=3, concat_axis=2, tiled=True)
    bands_dev = banded.shape[3] * FT // FB
    spec_bands = banded.reshape(2, realiz, width, bands_dev, FB)
    scale = 1.0 / (FB * realiz * lax.axis_size("real"))
    row_count = width // lax.axis_size("real")
    row_first = lax.axis_index("real") * row_count
    shard_piece = lax.all_gather(spec_bands, "real", axis=1, tiled=True)
    own_part = lax.dynamic_slice_in_dim(shard_piece, row_first, row_count, 2)
    return gram_parts(own_part, shard_piece) * scale


VMEM = pltpu.VMEM
BIG = 60 * 1024 * 1024


def step_order(parts):
    return sorted(range(1, parts), key=lambda step: (-min(step, parts - step), step))


def remote(here, there, sent, landed, target):
    copy = pltpu.make_async_remote_copy(
        src_ref=here,
        dst_ref=there,
        send_sem=sent,
        recv_sem=landed,
        device_id=target,
        device_id_type=pl.DeviceIdType.MESH,
    )
    copy.start()
    return copy


def kerr_terms_at(first, piece, k, list_s, coef, fld, terms):
    span = pl.ds(first, piece)
    bl, bm, bn = (list_s[k, 0, i] for i in (1, 2, 3))
    m_re, m_im = fld[0, bm, :, span][:, None], fld[1, bm, :, span][:, None]
    n_re, n_im = fld[0, bn, :, span][None], fld[1, bn, :, span][None]
    p_re = (m_re * n_re + m_im * n_im).reshape(MB * MB, piece)
    p_im = (m_im * n_re - m_re * n_im).reshape(MB * MB, piece)
    pairs = jnp.concatenate([p_re, p_im], axis=1).astype(jnp.bfloat16)
    w = jnp.dot(coef, pairs, preferred_element_type=jnp.float32)
    w_re = w[:, :piece].reshape(MB, MB, piece)
    w_im = w[:, piece:].reshape(MB, MB, piece)
    l_re, l_im = fld[0, bl, :, span][:, None], fld[1, bl, :, span][:, None]
    at = pl.ds(pl.multiple_of(k * MB, MB), MB)
    terms[0, at, span] = jnp.sum(w_re * l_re - w_im * l_im, axis=0)
    terms[1, at, span] = jnp.sum(w_re * l_im + w_im * l_re, axis=0)


def owner_table(blocks, width, list_s):
    shape = (width, blocks * MB)
    row = lax.broadcasted_iota(jnp.int32, shape, 0)
    col = lax.broadcasted_iota(jnp.int32, shape, 1)
    wanted = jnp.full(shape, -1, jnp.int32)
    for k in range(blocks):
        wanted = jnp.where(col // MB == k, list_s[k, 0, 0] * MB + col % MB, wanted)
    return (row == wanted).astype(jnp.float32).astype(jnp.bfloat16)


def whole_kernel(parts, sides, x_ref, coef_ref, list_ref, f1h, f1l, tw_re, tw_im, f2h, f2l,
                 out_ref, timed, coefs, swapped, lists, list_s, fld, terms, rows, stepped, by_mode, spec,
                 sends, recvs, own_sems):
    me = lax.axis_index("mode")
    other = {"real": 1 - lax.axis_index("real")}
    _, modes, times = x_ref.shape
    steps = times // parts
    width = parts * modes
    groups = width // MB
    fine = steps // FT
    pieces = min(2, fine)
    half = steps // pieces
    piece = min(half, 256)
    order = step_order(parts)
    barrier = pltpu.get_barrier_semaphore()
    for step in order:
        to = {"mode": lax.rem(me + step, parts)}
        pl.semaphore_signal(barrier, inc=1, device_id=to, device_id_type=pl.DeviceIdType.MESH)
    if sides > 1:
        pl.semaphore_signal(barrier, inc=1, device_id=other, device_id_type=pl.DeviceIdType.MESH)
    pl.semaphore_wait(barrier, parts - 1 + (sides > 1))

    def chunk(to, part):
        at = pl.multiple_of(to * steps + part * half, 128)
        return x_ref.at[:, :, pl.ds(at, half)]

    def landing(part):
        return timed.at[me, :, :, pl.ds(part * half, half)]

    small, field_copies = [], [[] for _ in range(pieces)]
    for step in order:
        to = lax.rem(me + step, parts)
        there = {"mode": to}
        small.append(remote(coef_ref, coefs.at[me], sends.at[0, step], recvs.at[0, step], there))
        small.append(remote(list_ref, lists.at[me], sends.at[1, step], recvs.at[1, step], there))
    for part, copies in enumerate(field_copies):
        for step in order:
            to = lax.rem(me + step, parts)
            copies.append(
                remote(
                    chunk(to, part),
                    landing(part),
                    sends.at[4 + part, step],
                    recvs.at[4 + part, step],
                    {"mode": to},
                )
            )
    for slot, (here, there) in enumerate(((coef_ref, coefs.at[me]), (list_ref, lists.at[me]))):
        copy = pltpu.make_async_copy(here, there, own_sems.at[slot])
        copy.start()
        small.append(copy)
    for part, copies in enumerate(field_copies):
        copy = pltpu.make_async_copy(chunk(me, part), landing(part), own_sems.at[4 + part])
        copy.start()
        copies.append(copy)
    for copy in small:
        copy.wait()
    copy = pltpu.make_async_copy(lists, list_s, own_sems.at[2])
    copy.start()
    copy.wait()
    blocks = coefs.shape[0]
    owners = owner_table(blocks, width, list_s)
    order_of = (MB * MB, MB * MB)
    row = lax.broadcasted_iota(jnp.int32, order_of, 0)
    col = lax.broadcasted_iota(jnp.int32, order_of, 1)
    swap = (col == (row % MB) * MB + row // MB).astype(jnp.float32).astype(jnp.bfloat16)
    for k in range(blocks):
        swapped[k] = jnp.dot(
            swap, coefs[k], preferred_element_type=jnp.float32
        ).astype(jnp.bfloat16)
    for part, copies in enumerate(field_copies):
        for copy in copies:
            copy.wait()
        span = pl.ds(part * half, half)
        for c in range(2):
            fld[c, :, :, span] = timed[:, c, :, span].astype(jnp.float32).reshape(groups, MB, half)

        def one_block(k, carry):
            coef = swapped[k]
            for at in range(part * half, (part + 1) * half, piece):
                kerr_terms_at(at, piece, k, list_s, coef, fld, terms)
            return carry

        lax.fori_loop(0, blocks, one_block, 0, unroll=2)
        for c in range(2):
            term = terms[1 - c, :, span]
            high = term.astype(jnp.bfloat16)
            low = (term - high.astype(jnp.float32)).astype(jnp.bfloat16)
            kerr = jnp.dot(owners, high, preferred_element_type=jnp.float32)
            kerr = kerr + jnp.dot(owners, low, preferred_element_type=jnp.float32)
            turn = kerr_strength * (2 * c - 1)
            new = fld[c, :, :, span].reshape(width, half) + turn * kerr
            for g in range(groups):
                for n in range(half // FT):
                    row = g * (MB * 2 * fine) + c * fine + part * (half // FT) + n
                    rows[pl.ds(row, MB, stride=2 * fine), :] = new[
                        g * MB : (g + 1) * MB, n * FT : (n + 1) * FT
                    ]
    stepped[...] = rows[...].astype(jnp.bfloat16).reshape(stepped.shape)

    mode_parts = min(2, modes // 2)
    few = modes // mode_parts
    mode_copies = []
    for part in range(mode_parts):
        some = pl.ds(part * few, few)
        copies = []
        for step in order:
            to = lax.rem(me + step, parts)
            copies.append(
                remote(
                    stepped.at[to, some],
                    by_mode.at[me, some],
                    sends.at[8 + part, step],
                    recvs.at[8 + part, step],
                    {"mode": to},
                )
            )
        copy = pltpu.make_async_copy(
            stepped.at[me, some], by_mode.at[me, some], own_sems.at[8 + part]
        )
        copy.start()
        mode_copies.append(copies + [copy])
    for part, copies in enumerate(mode_copies):
        for copy in copies:
            copy.wait()
        some = range(part * few, (part + 1) * few)
        dft_modes(some, by_mode, f1h, f1l, tw_re, tw_im, f2h, f2l, rows)
    spec[...] = rows[...].astype(jnp.bfloat16).reshape(spec.shape)

    pending, passed = [], []
    for step in order:
        to = lax.rem(me + step, parts)
        pending.append(
            (
                remote(spec.at[to], out_ref.at[0, me], sends.at[2, step], recvs.at[2, step], {"mode": to}),
                lax.rem(me - step + parts, parts),
            )
        )
    copy = pltpu.make_async_copy(spec.at[me], out_ref.at[0, me], own_sems.at[3])
    copy.start()
    if sides > 1:
        passed.append(remote(spec.at[me], out_ref.at[1, me], sends.at[3, 0], recvs.at[3, 0], other))
    for step, (arrival, source) in zip(order, pending):
        arrival.wait_recv()
        if sides > 1:
            passed.append(
                remote(
                    out_ref.at[0, source],
                    out_ref.at[1, source],
                    sends.at[3, step],
                    recvs.at[3, step],
                    other,
                )
            )
    copy.wait()
    for arrival, _ in pending:
        arrival.wait_send()
    for copy in passed:
        copy.wait()


def spectra_of(field, coef, listed, parts, sides):
    _, modes, times = field.shape
    steps = times // parts
    width = parts * modes
    fine = steps // FT
    half = jnp.bfloat16
    return pl.pallas_call(
        functools.partial(whole_kernel, parts, sides),
        out_shape=jax.ShapeDtypeStruct((sides, parts, fine, 2, modes, FT), half),
        in_specs=[pl.BlockSpec(memory_space=pl.ANY)] + [pl.BlockSpec(memory_space=VMEM)] * 8,
        out_specs=pl.BlockSpec(memory_space=VMEM),
        scratch_shapes=[
            VMEM((parts, 2, modes, steps), half),
            VMEM((parts,) + coef.shape, half),
            VMEM((parts,) + coef.shape, half),
            VMEM((parts,) + listed.shape, jnp.int32),
            pltpu.SMEM((parts,) + listed.shape, jnp.int32),
            VMEM((2, width // MB, MB, steps), jnp.float32),
            VMEM((2, parts * MB, steps), jnp.float32),
            VMEM((2 * width * fine, FT), jnp.float32),
            VMEM((parts, modes, 2 * fine, FT), half),
            VMEM((parts, modes, 2 * fine, FT), half),
            VMEM((parts, fine, 2, modes, FT), half),
            pltpu.SemaphoreType.DMA((12, parts)),
            pltpu.SemaphoreType.DMA((12, parts)),
            pltpu.SemaphoreType.DMA((12,)),
        ],
        compiler_params=pltpu.CompilerParams(
            collective_id=0, has_side_effects=True, vmem_limit_bytes=BIG
        ),
    )(field, coef, listed, *dft_tables(parts))


def dft_tables(parts):
    a = np.arange(FT)
    four = np.exp(-2j * np.pi / FT * (np.outer(a, a) % FT))
    twist = np.exp(-2j * np.pi / NT * (np.outer(a, a) % NT)) / FT
    real = np.block([[four.real, -four.imag], [four.imag, four.real]])
    first = real.reshape(2 * FT, 2, parts, FT // parts).transpose(0, 2, 1, 3)
    first = first.reshape(2 * FT, 2 * FT)
    second = real.reshape(2, FT, 2 * FT).transpose(1, 0, 2).reshape(2 * FT, 2 * FT)

    def split(t):
        t = t.astype(np.float32)
        high = t.astype(jnp.bfloat16)
        return high, (t - high.astype(np.float32)).astype(jnp.bfloat16)

    return (
        *split(first),
        twist.real.astype(np.float32),
        twist.imag.astype(np.float32),
        *split(second),
    )


def dft_modes(some, x_ref, f1h, f1l, tw_re, tw_im, f2h, f2l, rows):
    modes = x_ref.shape[1]
    nt = (((1,), (1,)), ((), ()))
    dot = functools.partial(jnp.dot, preferred_element_type=jnp.float32)
    dot_nt = functools.partial(
        lax.dot_general, dimension_numbers=nt, preferred_element_type=jnp.float32
    )
    for m in some[::2]:
        x = jnp.concatenate(
            [x_ref[:, m].reshape(2 * FT, FT), x_ref[:, m + 1].reshape(2 * FT, FT)], axis=1
        )
        half = dot(f1h[...], x) + dot(f1l[...], x)
        turned = []
        for i in range(2):
            h_re, h_im = half[:FT, i * FT : (i + 1) * FT], half[FT:, i * FT : (i + 1) * FT]
            turned.append(
                jnp.concatenate(
                    [
                        h_re * tw_re[...] - h_im * tw_im[...],
                        h_re * tw_im[...] + h_im * tw_re[...],
                    ],
                    axis=1,
                )
            )
        turned = jnp.concatenate(turned, axis=0)
        high = turned.astype(jnp.bfloat16)
        low = (turned - high.astype(jnp.float32)).astype(jnp.bfloat16)
        out = dot_nt(f2h[...], high) + dot_nt(f2h[...], low) + dot_nt(f2l[...], high)
        for i in range(2):
            rows[pl.ds(m + i, 2 * FT, stride=modes), :] = out[:, i * FT : (i + 1) * FT]


def gram_kernel(scale, half_ref, spec_ref, out_ref):
    sides, parts, _, _, modes, _ = spec_ref.shape
    row_count = out_ref.shape[2]
    sources = row_count // modes
    first = half_ref[0] * sources
    cols, rows_re, rows_im = [], [], []
    for side in range(sides):
        re, im = (spec_ref[side, :, 0, c].reshape(parts * modes, FT) for c in range(2))
        own = pl.ds(first, sources)
        own_re, own_im = (spec_ref[side, own, 0, c].reshape(row_count, FT) for c in range(2))
        cols += [re, im]
        rows_re += [own_re, own_im]
        rows_im += [own_im, -own_re]
    cols = jnp.concatenate(cols, axis=1)
    rows = jnp.concatenate(
        [jnp.concatenate(rows_re, axis=1), jnp.concatenate(rows_im, axis=1)], axis=0
    )
    lane = lax.broadcasted_iota(jnp.int32, rows.shape, 1)
    band = (lane % FT) // FB
    for g in range(FT // FB):
        kept = jnp.where(band == g, rows, jnp.zeros_like(rows))
        out = lax.dot_general(
            kept, cols, (((1,), (1,)), ((), ())), preferred_element_type=jnp.float32
        )
        out_ref[g] = (out * scale).reshape(2, row_count, parts * modes)


def gram(half, spectra, row_count, scale):
    sides, parts, high, _, modes, _ = spectra.shape
    width = parts * modes
    per = FT // FB
    return pl.pallas_call(
        functools.partial(gram_kernel, scale),
        grid=(high,),
        out_shape=jax.ShapeDtypeStruct((high * per, 2, row_count, width), jnp.float32),
        in_specs=[
            pl.BlockSpec(memory_space=pltpu.SMEM),
            pl.BlockSpec((sides, parts, 1, 2, modes, FT), lambda j: (0, 0, j, 0, 0, 0)),
        ],
        out_specs=pl.BlockSpec((per, 2, row_count, width), lambda j: (j, 0, 0, 0)),
        compiler_params=pltpu.CompilerParams(vmem_limit_bytes=BIG),
    )(half, spectra)


def tiled_shards(input_field, kerr_coeff, block_list):
    parts, sides = lax.axis_size("mode"), lax.axis_size("real")
    _, _, modes, times = input_field.shape
    width = parts * modes
    spectra = spectra_of(
        input_field.reshape(2, modes, times), kerr_coeff[0], block_list, parts, sides
    )
    half = lax.axis_index("real").astype(jnp.int32).reshape(1)
    return gram(half, spectra, width // sides, 1.0 / (FB * sides))


def tiles_fit(mesh):
    parts = mesh.shape["mode"]
    return FT % parts == 0 and (2 * FT // parts) % 16 == 0 and mesh.shape["real"] <= 2


def either(mesh, input_field, kerr_coeff, block_list):
    modes = input_field.shape[2]
    blocks_each = kerr_coeff.shape[0]
    fits = tiles_fit(mesh) and modes % 16 == 0 and blocks_each == 1
    fits = fits and input_field.shape[1] == 1 and input_field.shape[3] == NT
    return (tiled_shards if fits else shards)(input_field, kerr_coeff, block_list)


def solution(mesh):
    return jax.shard_map(
        functools.partial(either, mesh),
        mesh=mesh,
        in_specs=(P(None, "real", "mode", None), P("mode", None, None), P("mode", None)),
        out_specs=P("mode", None, "real", None),
        check_vma=False,
    )
```
